256 devices in a mesh: gx: 16 (over z_lo, x), gy: 2 (over core), gz: 8 (over z_hi, y).
Axes of the slice: x: 4, y: 4, z: 8 (z_hi: 2, z_lo: 4; z = z_hi * 4 + z_lo), core: 2. Of those that a mesh axis runs over, the one named last changes fastest.
Arguments:
- tokens: bfloat16 [128, 32, 128, 192], P('gx', 'gy', 'gz'), may hold values from -6 to 6
- upstream: bfloat16 [128, 32, 128, 192], P('gx', 'gy', 'gz'), may hold values from -6 to 6
- norm_gain: float32 [192], replicated, may hold values from 0.25 to 1.75
- norm_bias: float32 [192], replicated, may hold values from -3 to 3
- qkv_weight: bfloat16 [192, 576], replicated, may hold values from -4 to 4, as said below
- qkv_bias: float32 [576], replicated, may hold values from -3 to 3
- proj_weight: bfloat16 [192, 192], replicated, may hold values from -0.4375 to 0.4375
Outputs:
- token_grad: bfloat16 [128, 32, 128, 192], P('gx', 'gy', 'gz')
- qkv_weight_grad: float32 [192, 576], replicated
- qkv_bias_grad: float32 [576], replicated
- proj_weight_grad: float32 [192, 192], replicated
- proj_bias_grad: float32 [192], replicated
- gain_grad: float32 [192], replicated
- norm_bias_grad: float32 [192], replicated
The draws below stay inside these ranges and needn't reach their ends.
Inputs may be any that keep to these rules, and one draw needn't show every extreme that they name: `qkv_weight`: columns are the query, key and value projections in that order, each 6 heads of 32 columns.
All inputs are finite; a program needn't handle non-finite values.
Results may differ from the reference program's by a relative error of at most 0.02.
The reference program's roundings to bfloat16 on the way (of `hidden`, `packed`, `probs_half`, `attended`, `attended_grad`, `score_grad` and `packed_grad`) count: a program that leaves them out, or rounds other values in their place, can miss the bound.
Values may be sent and summed in bfloat16 or wider, within the bound.
No kernel may reach another device: no remote copies, remote signals or barrier semaphores. Data moves between devices by JAX's collectives and lax.ppermute only.
A program may use at most 64 MiB of HBM per device.

```python
import jax
import jax.numpy as jnp
from jax import lax

C = 192
HEADS = 6
HEAD_DIM = 32
WIN = 8
SHIFT = 4
NX = 128
NY = 32
NZ = 128
TOKENS = 524288


def draw_qkv_weight(key, part):
    base = jax.random.normal(key, (C, 3 * C), jnp.float32) * C ** (-0.5)
    return jnp.clip(base, -4.0, 4.0).astype(jnp.bfloat16)


def spiked(entries, own_key, source, target, blocks, factor):
    owner, partner = [(jnp.arange(entries.shape[dim]) // (entries.shape[dim] // blocks)).reshape([-1 if axis == dim else 1 for axis in range(entries.ndim)]) for dim in (source, target)]
    chosen = jax.random.permutation(own_key, blocks)[partner]
    strong = (owner == chosen) | (owner == (partner + blocks // 2) % blocks)
    return jnp.where(strong, factor * entries, entries)


def block_scale(own_key, dims, pieces, low, largest):
    def one(position, blocks):
        steps = jax.random.uniform(jax.random.fold_in(jax.random.fold_in(own_key, 6), position), (blocks,), jnp.float32, low / len(pieces), largest / len(pieces))
        return jnp.repeat(jnp.exp(steps), dims[position] // blocks).reshape((-1,) + (1,) * (len(dims) - position - 1))

    level = one(*pieces[0])
    for cut in pieces[1:]:
        level = level * one(*cut)
    return level


def gaussian(own_key, dims, scale, most, split=(), kind=jnp.bfloat16):
    drawn = scale * jax.random.normal(own_key, dims, jnp.float32)
    if split:
        drawn = drawn * block_scale(own_key, dims, split, -0.22, 0.18)
    return jnp.clip(drawn, -most, most).astype(kind)


def heavy_noise(key, dims, scale, limit, pieces, heavy, held_as=jnp.bfloat16):
    entries = scale * jax.random.normal(key, dims, jnp.float32)
    if pieces:
        entries = entries * block_scale(key, dims, pieces, -0.22, 0.18)
    return jnp.clip(spiked(entries, jax.random.fold_in(key, 3), *heavy), -limit, limit).astype(held_as)


def setup_inputs(seed: int = 0) -> dict:
    streams_of = jax.random.split(jax.random.key(seed), 8)
    return {
        "tokens": gaussian(streams_of[0], (NX, NY, NZ, C), 1.0, 6.0, ((0, 16), (1, 2), (2, 8))),
        "upstream": heavy_noise(streams_of[1], (NX, NY, NZ, C), 1.0, 6.0, ((0, 16), (1, 2), (2, 8)), (0, 3, 16, 2.0)),
        "norm_gain": jnp.clip(1.0 + 0.15 * jax.random.normal(streams_of[2], (C,), jnp.float32), 0.25, 1.75),
        "norm_bias": gaussian(streams_of[3], (C,), 0.5, 3.0, (), jnp.float32),
        "qkv_weight": draw_qkv_weight(jax.random.fold_in(streams_of[7], 71), 0),
        "qkv_bias": gaussian(streams_of[5], (3 * C,), 0.5, 3.0, (), jnp.float32),
        "proj_weight": gaussian(streams_of[6], (C, C), C ** -0.5, 0.4375),
    }


def window_grads(tok, upward, idents, norm_gain, norm_bias, qkv_weight, qkv_bias, proj_weight):
    length = tok.shape[0]
    width = tok.shape[1]
    single = jnp.float32
    factor = HEAD_DIM ** (-0.5)
    inputs = tok.astype(single)
    centred = inputs - lax.optimization_barrier(jnp.mean(inputs, axis=-1, keepdims=True))
    inverse = lax.rsqrt(lax.optimization_barrier(jnp.mean(centred * centred, axis=-1, keepdims=True)) + 1e-05)
    normed = centred * inverse
    hidden = (normed * norm_gain + norm_bias).astype(jnp.bfloat16)
    packed = (jnp.dot(hidden, qkv_weight, preferred_element_type=single) + qkv_bias).astype(jnp.bfloat16)
    query = packed[:, :width].reshape(length, HEADS, HEAD_DIM).astype(single)
    keyset = packed[:, width:2 * width].reshape(length, HEADS, HEAD_DIM).astype(single)
    valset = packed[:, 2 * width:].reshape(length, HEADS, HEAD_DIM).astype(single)
    scores = jnp.einsum('qhd,khd->hqk', query, keyset) * factor
    same = idents[:, None] == idents[None, :]
    scores = jnp.where(same[None], scores, -1e+30)
    peak = lax.optimization_barrier(jnp.max(scores, axis=-1, keepdims=True))
    expo = jnp.exp(scores - peak)
    probs = expo / lax.optimization_barrier(jnp.sum(expo, axis=-1, keepdims=True))
    probs_half = probs.astype(jnp.bfloat16)
    attended = jnp.einsum('hqk,khd->qhd', probs_half.astype(single), valset).reshape(length, width).astype(jnp.bfloat16)
    up_single = upward.astype(single)
    grad_proj = jnp.dot(attended.T, upward, preferred_element_type=single)
    grad_pbias = lax.optimization_barrier(jnp.sum(up_single, axis=0))
    attended_grad = jnp.dot(upward, proj_weight.T, preferred_element_type=single).astype(jnp.bfloat16)
    attended_grad = attended_grad.reshape(length, HEADS, HEAD_DIM).astype(single)
    prob_grad = jnp.einsum('qhd,khd->hqk', attended_grad, valset)
    inner = lax.optimization_barrier(jnp.sum(probs * prob_grad, axis=-1, keepdims=True))
    score_grad = (probs * (prob_grad - inner) * factor).astype(jnp.bfloat16).astype(single)
    query_grad = jnp.einsum('hqk,khd->qhd', score_grad, keyset).reshape(length, width)
    key_grad = jnp.einsum('hqk,qhd->khd', score_grad, query).reshape(length, width)
    value_grad = jnp.einsum('hqk,qhd->khd', probs_half.astype(single), attended_grad).reshape(length, width)
    packed_grad = jnp.concatenate([query_grad, key_grad, value_grad], axis=1).astype(jnp.bfloat16)
    grad_qkv = jnp.dot(hidden.T, packed_grad, preferred_element_type=single)
    grad_qbias = lax.optimization_barrier(jnp.sum(packed_grad.astype(single), axis=0))
    hidden_grad = jnp.dot(packed_grad, qkv_weight.T, preferred_element_type=single)
    grad_gain = lax.optimization_barrier(jnp.sum(hidden_grad * normed, axis=0))
    grad_nbias = lax.optimization_barrier(jnp.sum(hidden_grad, axis=0))
    normed_grad = hidden_grad * norm_gain
    first = lax.optimization_barrier(jnp.mean(normed_grad, axis=-1, keepdims=True))
    second = lax.optimization_barrier(jnp.mean(normed_grad * normed, axis=-1, keepdims=True))
    token_grad = (up_single + inverse * (normed_grad - first - normed * second)).astype(jnp.bfloat16)
    return (token_grad, (grad_qkv, grad_qbias, grad_proj, grad_pbias, grad_gain, grad_nbias))

def to_windows(block):
    sizes = block.shape[:3]
    rest = block.shape[3:]
    shaped = block.reshape((sizes[0] // WIN, WIN, sizes[1] // WIN, WIN, sizes[2] // WIN, WIN) + rest)
    order = (0, 2, 4, 1, 3, 5) + tuple(range(6, 6 + len(rest)))
    return shaped.transpose(order).reshape((-1, WIN ** 3) + rest)

def from_windows(wins, first, second, third):
    rest = wins.shape[2:]
    shaped = wins.reshape((first // WIN, second // WIN, third // WIN, WIN, WIN, WIN) + rest)
    order = (0, 3, 1, 4, 2, 5) + tuple(range(6, 6 + len(rest)))
    return shaped.transpose(order).reshape((first, second, third) + rest)

def window_index(total):
    placed = (jnp.arange(total, dtype=jnp.int32) + SHIFT) % total
    return ((placed + SHIFT) // WIN, total // WIN + 1)

def reference(tokens, upstream, norm_gain, norm_bias, qkv_weight, qkv_bias, proj_weight):
    rolled = jnp.roll(tokens, (-SHIFT, -SHIFT, -SHIFT), axis=(0, 1, 2))
    rolled_up = jnp.roll(upstream, (-SHIFT, -SHIFT, -SHIFT), axis=(0, 1, 2))
    index_x, span_x = window_index(NX)
    index_y, span_y = window_index(NY)
    index_z, span_z = window_index(NZ)
    idents = (index_x[:, None, None] * span_y + index_y[None, :, None]) * span_z + index_z[None, None, :]
    token_wins = to_windows(rolled)
    up_wins = to_windows(rolled_up)
    ident_wins = to_windows(idents.astype(jnp.int32))
    width = tokens.shape[3]
    zeros = (jnp.zeros((width, 3 * width), jnp.float32), jnp.zeros((3 * width,), jnp.float32), jnp.zeros((width, width), jnp.float32), jnp.zeros((width,), jnp.float32), jnp.zeros((width,), jnp.float32), jnp.zeros((width,), jnp.float32))

    def advance(carry, item):
        grad_win, parts = window_grads(item[0], item[1], item[2], norm_gain, norm_bias, qkv_weight, qkv_bias, proj_weight)
        return (tuple((old + new for old, new in zip(carry, parts))), grad_win)
    totals, grad_wins = lax.scan(advance, zeros, (token_wins, up_wins, ident_wins))
    token_grad = from_windows(grad_wins, NX, NY, NZ)
    factor = float(TOKENS) ** (-0.5)
    return (token_grad, totals[0] * factor, totals[1] * factor, totals[2] * factor, totals[3] * factor, totals[4] * factor, totals[5] * factor)
```

```python
import functools
import math

import jax
import jax.numpy as jnp
from jax import lax
from jax.experimental import pallas as pl
from jax.experimental.pallas import tpu as pltpu
from jax.sharding import Mesh, PartitionSpec as P

HEADS = 6
WIN = 8
SHIFT = 4
FAR = -1e30
LANES = 128
F32 = jnp.float32
BF16 = jnp.bfloat16


def dot(a, b):
    return jnp.dot(a, b, preferred_element_type=F32)


def dot_rows(a, b):
    return lax.dot_general(a, b, (((1,), (1,)), ((), ())), preferred_element_type=F32)


def dot_cols(a, b):
    return lax.dot_general(a, b, (((0,), (0,)), ((), ())), preferred_element_type=F32)


def window_kernel(
    flags, tok, up, gain, nbias, w_cols, w_rows, qbias, proj,
    out, grads, acc_qkv, acc_proj, acc_gain, acc_nb, packed_grad, attended,
):
    step = pl.program_id(0)
    width = w_rows.shape[0]
    count = WIN**3
    size = width // HEADS
    factor = size**-0.5
    scale = factor * math.log2(math.e)

    @pl.when(step == 0)
    def _():
        acc_qkv[...] = jnp.zeros_like(acc_qkv)
        acc_proj[...] = jnp.zeros_like(acc_proj)
        acc_gain[...] = jnp.zeros_like(acc_gain)
        acc_nb[...] = jnp.zeros_like(acc_nb)
        attended[...] = jnp.ones_like(attended)

    upward = up[...].astype(F32).reshape(count, width)
    upward_half = upward.astype(BF16)
    inputs = tok[...].astype(F32).reshape(count, width).T
    centred = inputs - jnp.mean(inputs, axis=0, keepdims=True)
    inverse = lax.rsqrt(jnp.mean(centred * centred, axis=0, keepdims=True) + 1e-5)
    normed = centred * inverse
    hidden = (normed * gain[...] + nbias[...]).astype(BF16)
    packed = (dot(w_cols[...], hidden) + qbias[...]).astype(BF16)
    att_grad = dot_rows(proj[...], upward_half).astype(BF16)

    last = (step == pl.num_programs(0) - 1).astype(jnp.int32)
    place = lax.broadcasted_iota(jnp.int32, (16, count), 1)
    row = lax.broadcasted_iota(jnp.int32, (16, count), 0)
    code = (
        4 * flags[0] * ((place >> 8) & 1)
        + 2 * flags[1] * last * ((place >> 5) & 1)
        + flags[2] * ((place >> 2) & 1)
    )
    same = code == row
    query_code = jnp.where(same, 1.0, 0.0).astype(BF16)
    key_code = jnp.where(same, 0.0, FAR).astype(BF16)
    ones = jnp.ones((16, count), BF16)

    for head in range(HEADS):
        lo = size * head
        at_q = slice(lo, lo + size)
        at_k = slice(width + lo, width + lo + size)
        at_v = slice(2 * width + lo, 2 * width + lo + size)
        query, keyset, valset, grad = packed[at_q], packed[at_k], packed[at_v], att_grad[at_q]
        value_ones = jnp.concatenate([valset, ones], axis=0)
        scores = dot_cols(
            jnp.concatenate([keyset, key_code], axis=0),
            jnp.concatenate([query, query_code], axis=0),
        )
        peak = jnp.max(scores, axis=0, keepdims=True)
        expo = jnp.exp2(scores * scale - peak * scale).astype(BF16)
        mixed = dot(value_ones, expo)
        recip = 1.0 / mixed[size : size + 1]
        result = mixed[:size] * recip
        attended[at_q, :] = result.astype(BF16)
        grad_scaled = (grad.astype(F32) * recip).astype(BF16)
        inner = jnp.sum(grad_scaled.astype(F32) * result, axis=0, keepdims=True)
        inner_high = inner.astype(BF16).astype(F32)
        inner_rows = jnp.where(
            row == 0, -inner_high, jnp.where(row == 1, inner_high - inner, 0.0)
        ).astype(BF16)
        spread = dot_cols(value_ones, jnp.concatenate([grad_scaled, inner_rows], axis=0))
        score_grad = expo * spread.astype(BF16)
        packed_grad[at_q, :] = (dot(keyset, score_grad) * factor).astype(BF16)
        packed_grad[at_k, :] = (dot_rows(query, score_grad) * factor).astype(BF16)
        packed_grad[at_v, :] = dot_rows(grad_scaled, expo).astype(BF16)

    grad_half = packed_grad[...]
    acc_qkv[...] += dot_rows(jnp.concatenate([hidden, ones], axis=0), grad_half)
    acc_proj[...] += dot(attended[...], upward_half)
    hidden_grad = dot(w_rows[...], grad_half)
    acc_gain[...] += hidden_grad * normed
    acc_nb[...] += hidden_grad
    normed_grad = hidden_grad * gain[...]
    first = jnp.mean(normed_grad, axis=0, keepdims=True)
    second = jnp.mean(normed_grad * normed, axis=0, keepdims=True)
    change = inverse * (normed_grad - first - normed * second)
    out[...] = (upward + change.T).reshape(out.shape).astype(BF16)

    @pl.when(step == pl.num_programs(0) - 1)
    def _():
        def put(at, value):
            grads[at : at + value.shape[0], : value.shape[1]] = value

        def over_tokens(value):
            folded = value[:, :LANES]
            for j in range(1, count // LANES):
                folded = folded + value[:, j * LANES : (j + 1) * LANES]
            return jnp.sum(folded.T, axis=0, keepdims=True)

        qkv = acc_qkv[...]
        prj = acc_proj[...]
        for j in range(4):
            put(width * j, qkv[:width, j * LANES : (j + 1) * LANES])
        put(width * 4, prj[:width, :LANES])
        put(
            width * 5,
            jnp.concatenate([qkv[:width, 4 * LANES :], prj[:width, LANES:]], axis=1),
        )
        grads[width * 6 :, :] = jnp.zeros_like(grads[width * 6 :, :])
        base = width * 6
        for j in range(5):
            put(base + j, qkv[width : width + 1, j * LANES : (j + 1) * LANES])
        small = [prj[width : width + 1], over_tokens(acc_gain[...]), over_tokens(acc_nb[...])]
        for j, value in enumerate(small):
            put(base + 8 + 2 * j, value[:, :LANES])
            put(base + 9 + 2 * j, value[:, LANES:])


def windows(flags, tok, up, weights, rows):
    depth, width_y, depth_z, width = tok.shape
    count = WIN**3
    block = pl.BlockSpec((WIN, WIN, WIN, width), lambda i: (0, i, 0, 0))
    whole = lambda *shape: pl.BlockSpec(shape, lambda i: (0,) * len(shape))
    return pl.pallas_call(
        window_kernel,
        grid=(width_y // WIN,),
        in_specs=[pl.BlockSpec(memory_space=pltpu.SMEM), block, block]
        + [whole(*value.shape) for value in weights],
        out_specs=[block, whole(rows, LANES)],
        out_shape=[
            jax.ShapeDtypeStruct(tok.shape, BF16),
            jax.ShapeDtypeStruct((rows, LANES), F32),
        ],
        scratch_shapes=[
            pltpu.VMEM((width + 16, 3 * width), F32),
            pltpu.VMEM((width + 16, width), F32),
            pltpu.VMEM((width, count), F32),
            pltpu.VMEM((width, count), F32),
            pltpu.VMEM((3 * width, count), BF16),
            pltpu.VMEM((width + 16, count), BF16),
        ],
        compiler_params=pltpu.CompilerParams(vmem_limit_bytes=48 * 2**20),
        name="window_grads",
    )(flags, tok, up, *weights)


def swapped(value, axis, bit):
    count = lax.axis_size(axis)
    return lax.ppermute(value, axis, [(a, a ^ bit) for a in range(count)])


def halve(value, axis, bit):
    half = value.shape[0] // 2
    upper = (lax.axis_index(axis) // bit) % 2
    pair = value.reshape((2, half) + value.shape[1:])
    kept = lax.dynamic_index_in_dim(pair, upper, 0, keepdims=False)
    given = lax.dynamic_index_in_dim(pair, 1 - upper, 0, keepdims=False)
    return kept + swapped(given, axis, bit)


def join(value, axis, bit):
    upper = (lax.axis_index(axis) // bit) % 2
    other = swapped(value, axis, bit)
    return jnp.where(
        upper == 0,
        jnp.concatenate([value, other], axis=0),
        jnp.concatenate([other, value], axis=0),
    )


def bits_of(axis):
    return [1 << j for j in range(lax.axis_size(axis).bit_length() - 1)]


def summed_everywhere(value):
    for axis in ("c", "y"):
        for bit in bits_of(axis):
            value = halve(value, axis, bit)
    for axis in ("x", "zl", "zh"):
        for bit in bits_of(axis):
            value = value + swapped(value, axis, bit)
    for axis in ("y", "c"):
        for bit in reversed(bits_of(axis)):
            value = join(value, axis, bit)
    return value


def passed_back(value, axes):
    sizes = [lax.axis_size(axis) for axis in axes]
    count = math.prod(sizes)
    return lax.ppermute(value, axes, [(a, (a - 1) % count) for a in range(count)])


def passed_back_both(value, first, second):
    ones = [lax.axis_size(axis) for axis in first]
    twos = [lax.axis_size(axis) for axis in second]
    n, m = math.prod(ones), math.prod(twos)
    pairs = [
        (a * m + b, ((a - 1) % n) * m + (b - 1) % m) for a in range(n) for b in range(m)
    ]
    return lax.ppermute(value, first + second, pairs)


def per_device(tokens, upstream, norm_gain, norm_bias, qkv_weight, qkv_bias, proj_weight):
    gx, gy, gz = ("zl", "x"), ("c",), ("zh", "y")
    width = tokens.shape[3]
    both = jnp.stack([tokens, upstream])
    came = passed_back(both[:, :, :SHIFT], gy)
    both = jnp.concatenate([both[:, :, SHIFT:], came], axis=2)
    came_x = passed_back(both[:, :SHIFT, :, SHIFT:], gx)
    came_z = passed_back(both[:, SHIFT:, :, :SHIFT], gz)
    came_xz = passed_back_both(both[:, :SHIFT, :, :SHIFT], gx, gz)
    near = jnp.concatenate([both[:, SHIFT:, :, SHIFT:], came_x], axis=1)
    rear = jnp.concatenate([came_z, came_xz], axis=1)
    half_a = near[:, :, :, :WIN]
    half_b = jnp.concatenate([near[:, :, :, WIN:], rear], axis=3)

    def is_last(axes):
        at = jnp.int32(0)
        count = 1
        for axis in axes:
            at = at * lax.axis_size(axis) + lax.axis_index(axis)
            count *= lax.axis_size(axis)
        return (at == count - 1).astype(jnp.int32)

    last_x, last_y, last_z = is_last(gx), is_last(gy), is_last(gz)
    weights = (
        norm_gain.reshape(-1, 1),
        norm_bias.reshape(-1, 1),
        qkv_weight.T,
        qkv_weight,
        qkv_bias.reshape(-1, 1),
        proj_weight,
    )
    rows = 6 * width + 64
    out_a, grads_a = windows(
        jnp.stack([last_x, last_y, 0 * last_z]), half_a[0], half_a[1], weights, rows
    )
    out_b, grads_b = windows(
        jnp.stack([last_x, last_y, last_z]), half_b[0], half_b[1], weights, rows
    )
    token_grad = jnp.concatenate([out_a, out_b], axis=2)
    total = summed_everywhere(grads_a + grads_b)
    devices = math.prod(lax.axis_size(axis) for axis in gx + gy + gz)
    total = total * float(math.prod(tokens.shape[:3]) * devices) ** (-0.5)
    parts = [total[width * j : width * (j + 1)] for j in range(6)]
    half = width - LANES
    qkv_grad = jnp.concatenate(parts[:4] + [parts[5][:, :half]], axis=1)
    proj_grad = jnp.concatenate([parts[4], parts[5][:, half:]], axis=1)
    small = total[6 * width :]
    flat = small.reshape(-1)
    at = 8 * LANES
    return (
        token_grad,
        qkv_grad,
        flat[: 3 * width],
        proj_grad,
        flat[at : at + width],
        flat[at + 2 * LANES : at + 2 * LANES + width],
        flat[at + 4 * LANES : at + 4 * LANES + width],
    )


def solution(mesh):
    split = Mesh(mesh.devices.reshape(4, 4, 2, 2, 4), ("zl", "x", "c", "zh", "y"))
    block = P(("zl", "x"), "c", ("zh", "y"), None)
    return jax.shard_map(
        per_device,
        mesh=split,
        in_specs=(block, block, P(), P(), P(), P(), P()),
        out_specs=(block, P(), P(), P(), P(), P(), P()),
        check_vma=False,
    )
```

```python
import functools
import math

import jax
import jax.numpy as jnp
from jax import lax
from jax.experimental import pallas as pl
from jax.experimental.pallas import tpu as pltpu
from jax.sharding import Mesh, PartitionSpec as P

HEADS = 6
WIN = 8
SHIFT = 4
FAR = -1e30
LANES = 128
PARTS = 8
MAIN = 144
ROWS = MAIN + 8
F32 = jnp.float32
BF16 = jnp.bfloat16


def dot(a, b):
    return jnp.dot(a, b, preferred_element_type=F32)


def dot_rows(a, b):
    return lax.dot_general(a, b, (((1,), (1,)), ((), ())), preferred_element_type=F32)


def dot_cols(a, b):
    return lax.dot_general(a, b, (((0,), (0,)), ((), ())), preferred_element_type=F32)


def window_kernel(
    flags, both, gain, nbias, w_cols, w_rows, qbias, proj,
    out, grads, acc_qkv, acc_proj, acc_gain, acc_nb, packed_grad, attended,
):
    step = pl.program_id(0)
    width = w_rows.shape[0]
    count = WIN**3
    size = width // HEADS
    factor = size**-0.5
    scale = factor * math.log2(math.e)

    @pl.when(step == 0)
    def _():
        acc_qkv[...] = jnp.zeros_like(acc_qkv)
        acc_proj[...] = jnp.zeros_like(acc_proj)
        acc_gain[...] = jnp.zeros_like(acc_gain)
        acc_nb[...] = jnp.zeros_like(acc_nb)
        attended[...] = jnp.ones_like(attended)

    arrived = both[...].astype(F32).reshape(count, 2 * width)
    upward = arrived[:, :width]
    upward_half = upward.astype(BF16)
    inputs = arrived[:, LANES:].T[width - LANES :]
    centred = inputs - jnp.mean(inputs, axis=0, keepdims=True)
    inverse = lax.rsqrt(jnp.mean(centred * centred, axis=0, keepdims=True) + 1e-5)
    normed = centred * inverse
    hidden = (normed * gain[...] + nbias[...]).astype(BF16)
    packed = (dot(w_cols[...], hidden) + qbias[...]).astype(BF16)
    att_grad = dot_rows(proj[...], upward_half).astype(BF16)

    last = (step == pl.num_programs(0) - 1).astype(jnp.int32)
    place = lax.broadcasted_iota(jnp.int32, (16, count), 1)
    row = lax.broadcasted_iota(jnp.int32, (16, count), 0)
    code = (
        4 * flags[0] * ((place >> 8) & 1)
        + 2 * flags[1] * last * ((place >> 5) & 1)
        + flags[2] * ((place >> 2) & 1)
    )
    same = code == row
    query_code = jnp.where(same, 1.0, 0.0).astype(BF16)
    key_code = jnp.where(same, 0.0, FAR).astype(BF16)
    ones = jnp.ones((16, count), BF16)

    for head in range(HEADS):
        lo = size * head
        at_q = slice(lo, lo + size)
        at_k = slice(width + lo, width + lo + size)
        at_v = slice(2 * width + lo, 2 * width + lo + size)
        query, keyset, valset, grad = packed[at_q], packed[at_k], packed[at_v], att_grad[at_q]
        value_ones = jnp.concatenate([valset, ones], axis=0)
        scores = dot_cols(
            jnp.concatenate([keyset, key_code], axis=0),
            jnp.concatenate([query, query_code], axis=0),
        )
        peak = jnp.max(scores, axis=0, keepdims=True)
        expo = jnp.exp2(scores * scale - peak * scale).astype(BF16)
        mixed = dot(value_ones, expo)
        recip = 1.0 / mixed[size : size + 1]
        result = mixed[:size] * recip
        attended[at_q, :] = result.astype(BF16)
        grad_scaled = (grad.astype(F32) * recip).astype(BF16)
        inner = jnp.sum(grad_scaled.astype(F32) * result, axis=0, keepdims=True)
        inner_high = inner.astype(BF16).astype(F32)
        inner_rows = jnp.where(
            row == 0, -inner_high, jnp.where(row == 1, inner_high - inner, 0.0)
        ).astype(BF16)
        spread = dot_cols(value_ones, jnp.concatenate([grad_scaled, inner_rows], axis=0))
        score_grad = expo * spread.astype(BF16)
        packed_grad[at_q, :] = (dot(keyset, score_grad) * factor).astype(BF16)
        packed_grad[at_k, :] = (dot_rows(query, score_grad) * factor).astype(BF16)
        packed_grad[at_v, :] = dot_rows(grad_scaled, expo).astype(BF16)

    grad_half = packed_grad[...]
    acc_qkv[...] += dot_rows(jnp.concatenate([hidden, ones], axis=0), grad_half)
    acc_proj[...] += dot(attended[...], upward_half)
    hidden_grad = dot(w_rows[...], grad_half)
    acc_gain[...] += hidden_grad * normed
    acc_nb[...] += hidden_grad
    normed_grad = hidden_grad * gain[...]
    first = jnp.mean(normed_grad, axis=0, keepdims=True)
    second = jnp.mean(normed_grad * normed, axis=0, keepdims=True)
    change = inverse * (normed_grad - first - normed * second)
    out[...] = (upward + change.T).reshape(out.shape).astype(BF16)

    @pl.when(step == pl.num_programs(0) - 1)
    def _():
        def put(at, value):
            done = 0
            while done < value.shape[0]:
                part, inside = divmod(at + done, MAIN)
                rows = min(value.shape[0] - done, MAIN - inside)
                grads[part, inside : inside + rows, :] = value[done : done + rows]
                done += rows

        def put_small(at, value):
            grads[at // 2, MAIN + at % 2, : value.shape[1]] = value[0]

        def over_tokens(value):
            folded = value[:, :LANES]
            for j in range(1, count // LANES):
                folded = folded + value[:, j * LANES : (j + 1) * LANES]
            return jnp.sum(folded.T, axis=0, keepdims=True)

        qkv = acc_qkv[...]
        prj = acc_proj[...]
        for j in range(4):
            put(width * j, qkv[:width, j * LANES : (j + 1) * LANES])
        put(width * 4, prj[:width, :LANES])
        put(
            width * 5,
            jnp.concatenate([qkv[:width, 4 * LANES :], prj[:width, LANES:]], axis=1),
        )
        grads[:, MAIN:, :] = jnp.zeros_like(grads[:, MAIN:, :])
        for j in range(5):
            put_small(j, qkv[width : width + 1, j * LANES : (j + 1) * LANES])
        small = [prj[width : width + 1], over_tokens(acc_gain[...]), over_tokens(acc_nb[...])]
        for j, value in enumerate(small):
            put_small(8 + 2 * j, value[:, :LANES])
            put_small(9 + 2 * j, value[:, LANES:])


def windows(flags, both, weights):
    depth, width_y, depth_z, wide = both.shape
    width = wide // 2
    count = WIN**3
    whole = lambda *shape: pl.BlockSpec(shape, lambda i: (0,) * len(shape))
    return pl.pallas_call(
        window_kernel,
        grid=(width_y // WIN,),
        in_specs=[
            pl.BlockSpec(memory_space=pltpu.SMEM),
            pl.BlockSpec((WIN, WIN, WIN, wide), lambda i: (0, i, 0, 0)),
        ]
        + [whole(*value.shape) for value in weights],
        out_specs=[
            pl.BlockSpec((WIN, WIN, WIN, width), lambda i: (0, i, 0, 0)),
            whole(PARTS, ROWS, LANES),
        ],
        out_shape=[
            jax.ShapeDtypeStruct((depth, width_y, depth_z, width), BF16),
            jax.ShapeDtypeStruct((PARTS, ROWS, LANES), F32),
        ],
        scratch_shapes=[
            pltpu.VMEM((width + 16, 3 * width), F32),
            pltpu.VMEM((width + 16, width), F32),
            pltpu.VMEM((width, count), F32),
            pltpu.VMEM((width, count), F32),
            pltpu.VMEM((3 * width, count), BF16),
            pltpu.VMEM((width + 16, count), BF16),
        ],
        compiler_params=pltpu.CompilerParams(vmem_limit_bytes=48 * 2**20),
        cost_estimate=pl.CostEstimate(
            flops=20 * 10**9, transcendentals=4 * 10**6, bytes_accessed=4 * 10**6
        ),
        name="window_grads",
    )(flags, both, *weights)


def swapped(value, axis, bit):
    count = lax.axis_size(axis)
    return lax.ppermute(value, axis, [(a, a ^ bit) for a in range(count)])


def coded(value):
    small = value[:, MAIN:]
    high = lax.reduce_precision(small, 8, 7)
    return jnp.concatenate([value[:, :MAIN], high, small - high], axis=1).astype(BF16)


def decoded(value):
    wide = value.astype(F32)
    small = wide[:, MAIN:ROWS] + wide[:, ROWS:]
    return jnp.concatenate([wide[:, :MAIN], small], axis=1)


def exchanged(value, axis, bit):
    return decoded(swapped(coded(value), axis, bit))


def halve(value, axis, bit):
    half = value.shape[0] // 2
    upper = (lax.axis_index(axis) // bit) % 2
    kept = lax.dynamic_slice_in_dim(value, upper * half, half, 0)
    given = lax.dynamic_slice_in_dim(value, (1 - upper) * half, half, 0)
    return kept + exchanged(given, axis, bit)


def join(value, axis, bit):
    upper = (lax.axis_index(axis) // bit) % 2
    other = swapped(value, axis, bit)
    return jnp.where(
        upper == 0,
        jnp.concatenate([value, other], axis=0),
        jnp.concatenate([other, value], axis=0),
    )


def bits_of(axis):
    return [1 << j for j in range(lax.axis_size(axis).bit_length() - 1)]


def summed_everywhere(value):
    for axis in ("c", "y"):
        for bit in bits_of(axis):
            value = halve(value, axis, bit)
    for axis in ("x", "zl", "zh"):
        for bit in bits_of(axis):
            value = value + exchanged(value, axis, bit)
    value = coded(value)
    for axis in ("y", "c"):
        for bit in reversed(bits_of(axis)):
            value = join(value, axis, bit)
    return decoded(value)


def passed_back(value, axes):
    sizes = [lax.axis_size(axis) for axis in axes]
    count = math.prod(sizes)
    return lax.ppermute(value, axes, [(a, (a - 1) % count) for a in range(count)])


def passed_back_both(value, first, second):
    ones = [lax.axis_size(axis) for axis in first]
    twos = [lax.axis_size(axis) for axis in second]
    n, m = math.prod(ones), math.prod(twos)
    pairs = [
        (a * m + b, ((a - 1) % n) * m + (b - 1) % m) for a in range(n) for b in range(m)
    ]
    return lax.ppermute(value, first + second, pairs)


def per_device(tokens, upstream, norm_gain, norm_bias, qkv_weight, qkv_bias, proj_weight):
    gx, gy, gz = ("zl", "x"), ("c",), ("zh", "y")
    width = tokens.shape[3]
    both = jnp.concatenate([upstream, tokens], axis=3)
    a_z, b_z = slice(SHIFT, SHIFT + WIN), slice(SHIFT + WIN, None)
    came_a = passed_back(both[:SHIFT, SHIFT:, a_z], gx)
    came_y = passed_back(both[:, :SHIFT], gy)
    came_ay = passed_back(came_y[:SHIFT, :, a_z], gx)
    both = jnp.concatenate([both[:, SHIFT:], came_y], axis=1)
    came_b = passed_back(both[:SHIFT, :, b_z], gx)
    came_z = passed_back(both[SHIFT:, :, :SHIFT], gz)
    came_xz = passed_back_both(both[:SHIFT, :, :SHIFT], gx, gz)
    far = jnp.concatenate([came_a, came_ay], axis=1)
    half_a = jnp.concatenate([both[SHIFT:, :, a_z], far], axis=0)
    half_b = jnp.concatenate(
        [
            jnp.concatenate([both[SHIFT:, :, b_z], came_b], axis=0),
            jnp.concatenate([came_z, came_xz], axis=0),
        ],
        axis=2,
    )

    def is_last(axes):
        at = jnp.int32(0)
        count = 1
        for axis in axes:
            at = at * lax.axis_size(axis) + lax.axis_index(axis)
            count *= lax.axis_size(axis)
        return (at == count - 1).astype(jnp.int32)

    last_x, last_y, last_z = is_last(gx), is_last(gy), is_last(gz)
    weights = (
        norm_gain.reshape(-1, 1),
        norm_bias.reshape(-1, 1),
        qkv_weight.T,
        qkv_weight,
        qkv_bias.reshape(-1, 1),
        proj_weight,
    )
    out_a, grads_a = windows(jnp.stack([last_x, last_y, 0 * last_z]), half_a, weights)
    out_b, grads_b = windows(jnp.stack([last_x, last_y, last_z]), half_b, weights)
    token_grad = jnp.concatenate([out_a, out_b], axis=2)
    total = summed_everywhere(grads_a + grads_b)
    devices = math.prod(lax.axis_size(axis) for axis in gx + gy + gz)
    total = total * float(math.prod(tokens.shape[:3]) * devices) ** (-0.5)
    main = total[:, :MAIN].reshape(-1, LANES)
    parts = [main[width * j : width * (j + 1)] for j in range(6)]
    half = width - LANES
    qkv_grad = jnp.concatenate(parts[:4] + [parts[5][:, :half]], axis=1)
    proj_grad = jnp.concatenate([parts[4], parts[5][:, half:]], axis=1)
    flat = total[:, MAIN : MAIN + 2].reshape(-1)
    at = 8 * LANES
    return (
        token_grad,
        qkv_grad,
        flat[: 3 * width],
        proj_grad,
        flat[at : at + width],
        flat[at + 2 * LANES : at + 2 * LANES + width],
        flat[at + 4 * LANES : at + 4 * LANES + width],
    )


def solution(mesh):
    split = Mesh(mesh.devices.reshape(4, 4, 2, 2, 4), ("zl", "x", "c", "zh", "y"))
    block = P(("zl", "x"), "c", ("zh", "y"), None)
    return jax.shard_map(
        per_device,
        mesh=split,
        in_specs=(block, block, P(), P(), P(), P(), P()),
        out_specs=(block, P(), P(), P(), P(), P(), P()),
        check_vma=False,
    )
```

```python
import functools
import math

import jax
import jax.numpy as jnp
from jax import lax
from jax.experimental import pallas as pl
from jax.experimental.pallas import tpu as pltpu
from jax.sharding import Mesh, PartitionSpec as P

HEADS = 6
WIN = 8
SHIFT = 4
FAR = -1e30
LANES = 128
PARTS = 8
MAIN = 144
ROWS = MAIN + 8
F32 = jnp.float32
BF16 = jnp.bfloat16


def dot(a, b):
    return jnp.dot(a, b, preferred_element_type=F32)


def dot_rows(a, b):
    return lax.dot_general(a, b, (((1,), (1,)), ((), ())), preferred_element_type=F32)


def dot_cols(a, b):
    return lax.dot_general(a, b, (((0,), (0,)), ((), ())), preferred_element_type=F32)


def window_kernel(
    flags, both, gain, nbias, w_cols, w_rows, qbias, proj,
    out, grads, acc_qkv, acc_proj, acc_gain, acc_nb, packed_grad, attended,
):
    step = pl.program_id(0)
    width = w_rows.shape[0]
    count = WIN**3
    size = width // HEADS
    factor = size**-0.5
    scale = factor * math.log2(math.e)

    @pl.when(step == 0)
    def _():
        acc_qkv[...] = jnp.zeros_like(acc_qkv)
        acc_proj[...] = jnp.zeros_like(acc_proj)
        acc_gain[...] = jnp.zeros_like(acc_gain)
        acc_nb[...] = jnp.zeros_like(acc_nb)
        attended[...] = jnp.ones_like(attended)

    arrived = both[...].astype(F32).reshape(count, 2 * width)
    upward = arrived[:, :width]
    upward_half = upward.astype(BF16)
    inputs = arrived[:, LANES:].T[width - LANES :]
    centred = inputs - jnp.mean(inputs, axis=0, keepdims=True)
    inverse = lax.rsqrt(jnp.mean(centred * centred, axis=0, keepdims=True) + 1e-5)
    normed = centred * inverse
    hidden = (normed * gain[...] + nbias[...]).astype(BF16)
    packed = (dot(w_cols[...], hidden) + qbias[...]).astype(BF16)
    att_grad = dot_rows(proj[...], upward_half).astype(BF16)

    last = (step == pl.num_programs(0) - 1).astype(jnp.int32)
    place = lax.broadcasted_iota(jnp.int32, (16, count), 1)
    row = lax.broadcasted_iota(jnp.int32, (16, count), 0)
    code = (
        4 * flags[0] * ((place >> 8) & 1)
        + 2 * flags[1] * last * ((place >> 5) & 1)
        + flags[2] * ((place >> 2) & 1)
    )
    same = code == row
    query_code = jnp.where(same, 1.0, 0.0).astype(BF16)
    key_code = jnp.where(same, 0.0, FAR).astype(BF16)
    ones = jnp.ones((16, count), BF16)

    def rows_of(kind, head):
        return slice(kind * width + size * head, kind * width + size * (head + 1))

    def score(head):
        return dot_cols(
            jnp.concatenate([packed[rows_of(1, head)], key_code], axis=0),
            jnp.concatenate([packed[rows_of(0, head)], query_code], axis=0),
        )

    def weigh(scores):
        peak = jnp.max(scores, axis=0, keepdims=True)
        return jnp.exp2((scores - peak) * scale).astype(BF16)

    def values(head):
        return jnp.concatenate([packed[rows_of(2, head)], ones], axis=0)

    def attend(head, expo):
        mixed = dot(values(head), expo)
        recip = 1.0 / mixed[size : size + 1]
        result = mixed[:size] * recip
        attended[rows_of(0, head), :] = result.astype(BF16)
        scaled = (att_grad[rows_of(0, head)].astype(F32) * recip).astype(BF16)
        inner = jnp.sum(scaled.astype(F32) * result, axis=0, keepdims=True)
        high = inner.astype(BF16).astype(F32)
        inner_rows = jnp.where(row == 0, -high, jnp.where(row == 1, high - inner, 0.0))
        return scaled, jnp.concatenate([scaled, inner_rows.astype(BF16)], axis=0)

    def pull_back(head, expo, scaled, spread):
        score_grad = expo * spread.astype(BF16)
        query, keyset = packed[rows_of(0, head)], packed[rows_of(1, head)]
        packed_grad[rows_of(2, head), :] = dot_rows(expo, scaled).T.astype(BF16)
        packed_grad[rows_of(0, head), :] = (dot(keyset, score_grad) * factor).astype(BF16)
        packed_grad[rows_of(1, head), :] = (dot_rows(score_grad, query).T * factor).astype(BF16)

    scores, earlier = score(0), None
    for head in range(HEADS + 1):
        following = score(head + 1) if head + 1 < HEADS else None
        expo = weigh(scores) if head < HEADS else None
        spread = None if earlier is None else dot_cols(values(head - 1), earlier[2])
        current = (expo, *attend(head, expo)) if head < HEADS else None
        if earlier is not None:
            pull_back(head - 1, earlier[0], earlier[1], spread)
        scores, earlier = following, current

    grad_half = packed_grad[...]
    acc_qkv[...] += dot_rows(jnp.concatenate([hidden, ones], axis=0), grad_half)
    acc_proj[...] += dot(attended[...], upward_half)
    hidden_grad = dot(w_rows[...], grad_half)
    acc_gain[...] += hidden_grad * normed
    acc_nb[...] += hidden_grad
    normed_grad = hidden_grad * gain[...]
    first = jnp.mean(normed_grad, axis=0, keepdims=True)
    second = jnp.mean(normed_grad * normed, axis=0, keepdims=True)
    change = inverse * (normed_grad - first - normed * second)
    out[...] = (upward + change.T).reshape(out.shape).astype(BF16)

    @pl.when(step == pl.num_programs(0) - 1)
    def _():
        def put(at, value):
            done = 0
            while done < value.shape[0]:
                part, inside = divmod(at + done, MAIN)
                rows = min(value.shape[0] - done, MAIN - inside)
                grads[part, inside : inside + rows, :] = value[done : done + rows]
                done += rows

        def put_small(at, value):
            grads[at // 2, MAIN + at % 2, : value.shape[1]] = value[0]

        def over_tokens(value):
            folded = value[:, :LANES]
            for j in range(1, count // LANES):
                folded = folded + value[:, j * LANES : (j + 1) * LANES]
            return jnp.sum(folded.T, axis=0, keepdims=True)

        qkv = acc_qkv[...]
        prj = acc_proj[...]
        for j in range(4):
            put(width * j, qkv[:width, j * LANES : (j + 1) * LANES])
        put(width * 4, prj[:width, :LANES])
        put(
            width * 5,
            jnp.concatenate([qkv[:width, 4 * LANES :], prj[:width, LANES:]], axis=1),
        )
        grads[:, MAIN:, :] = jnp.zeros_like(grads[:, MAIN:, :])
        for j in range(5):
            put_small(j, qkv[width : width + 1, j * LANES : (j + 1) * LANES])
        small = [prj[width : width + 1], over_tokens(acc_gain[...]), over_tokens(acc_nb[...])]
        for j, value in enumerate(small):
            put_small(8 + 2 * j, value[:, :LANES])
            put_small(9 + 2 * j, value[:, LANES:])


def windows(flags, both, weights):
    depth, width_y, depth_z, wide = both.shape
    width = wide // 2
    count = WIN**3
    whole = lambda *shape: pl.BlockSpec(shape, lambda i: (0,) * len(shape))
    return pl.pallas_call(
        window_kernel,
        grid=(width_y // WIN,),
        in_specs=[
            pl.BlockSpec(memory_space=pltpu.SMEM),
            pl.BlockSpec((WIN, WIN, WIN, wide), lambda i: (0, i, 0, 0)),
        ]
        + [whole(*value.shape) for value in weights],
        out_specs=[
            pl.BlockSpec((WIN, WIN, WIN, width), lambda i: (0, i, 0, 0)),
            whole(PARTS, ROWS, LANES),
        ],
        out_shape=[
            jax.ShapeDtypeStruct((depth, width_y, depth_z, width), BF16),
            jax.ShapeDtypeStruct((PARTS, ROWS, LANES), F32),
        ],
        scratch_shapes=[
            pltpu.VMEM((width + 16, 3 * width), F32),
            pltpu.VMEM((width + 16, width), F32),
            pltpu.VMEM((width, count), F32),
            pltpu.VMEM((width, count), F32),
            pltpu.VMEM((3 * width, count), BF16),
            pltpu.VMEM((width + 16, count), BF16),
        ],
        compiler_params=pltpu.CompilerParams(vmem_limit_bytes=48 * 2**20),
        cost_estimate=pl.CostEstimate(
            flops=20 * 10**9, transcendentals=4 * 10**6, bytes_accessed=4 * 10**6
        ),
        name="window_grads",
    )(flags, both, *weights)


def swapped(value, axis, bit):
    axes = (axis,) if isinstance(axis, str) else axis
    count = math.prod(lax.axis_size(name) for name in axes)
    return lax.ppermute(value, axis, [(a, a ^ bit) for a in range(count)])


def coded(value):
    small = value[:, MAIN:]
    high = lax.reduce_precision(small, 8, 7)
    return jnp.concatenate([value[:, :MAIN], high, small - high], axis=1).astype(BF16)


def decoded(value):
    wide = value.astype(F32)
    small = wide[:, MAIN:ROWS] + wide[:, ROWS:]
    return jnp.concatenate([wide[:, :MAIN], small], axis=1)


def halve(value, axis):
    half = value.shape[0] // 2
    upper = lax.axis_index(axis) % 2
    kept = lax.dynamic_slice_in_dim(value, upper * half, half, 0)
    given = lax.dynamic_slice_in_dim(value, (1 - upper) * half, half, 0)
    return kept + decoded(swapped(coded(given), axis, 1))


def quarter(value, axis):
    part = value.shape[0] // 4
    at = lax.axis_index(axis)
    sent = coded(value)
    total = lax.dynamic_slice_in_dim(value, at * part, part, 0)
    for bits in (2, 1, 3):
        given = lax.dynamic_slice_in_dim(sent, (at ^ bits) * part, part, 0)
        total = total + decoded(swapped(given, axis, bits))
    return total


def sum_of_two(value, axes, bit):
    sent = coded(value)
    return decoded(sent) + decoded(swapped(sent, axes, bit))


def sum_of_four(value, axes, first, second):
    sent = coded(value)
    both = swapped(sent, axes, first ^ second)
    one, two = swapped(sent, axes, first), swapped(sent, axes, second)
    return (decoded(sent) + decoded(one)) + (decoded(two) + decoded(both))


def join(value, axis):
    upper = lax.axis_index(axis) % 2 == 1
    other = swapped(value, axis, 1)
    return jnp.concatenate(
        [jnp.where(upper, other, value), jnp.where(upper, value, other)], axis=0
    )


def join_four(value, axis):
    at = lax.axis_index(axis)
    odd, upper = at % 2 == 1, at >= 2
    far, one, three = (swapped(value, axis, bits) for bits in (2, 1, 3))
    flat = [
        jnp.where(odd, one, value),
        jnp.where(odd, value, one),
        jnp.where(odd, three, far),
        jnp.where(odd, far, three),
    ]
    return jnp.concatenate([jnp.where(upper, flat[j ^ 2], flat[j]) for j in range(4)], axis=0)


def summed_everywhere(value):
    value = quarter(halve(value, "c"), "y")
    value = sum_of_four(value, ("x",), 1, 2)
    value = sum_of_two(value, ("zl", "zh"), 2)
    value = sum_of_four(value, ("zl", "zh"), 4, 1)
    return decoded(join(join_four(coded(value), "y"), "c"))


def passed_back(value, axes):
    sizes = [lax.axis_size(axis) for axis in axes]
    count = math.prod(sizes)
    return lax.ppermute(value, axes, [(a, (a - 1) % count) for a in range(count)])


def passed_back_both(value, first, second):
    ones = [lax.axis_size(axis) for axis in first]
    twos = [lax.axis_size(axis) for axis in second]
    n, m = math.prod(ones), math.prod(twos)
    pairs = [
        (a * m + b, ((a - 1) % n) * m + (b - 1) % m) for a in range(n) for b in range(m)
    ]
    return lax.ppermute(value, first + second, pairs)


def per_device(tokens, upstream, norm_gain, norm_bias, qkv_weight, qkv_bias, proj_weight):
    gx, gy, gz = ("zl", "x"), ("c",), ("zh", "y")
    width = tokens.shape[3]
    both = jnp.concatenate([upstream, tokens], axis=3)
    a_z, b_z = slice(SHIFT, SHIFT + WIN), slice(SHIFT + WIN, None)
    came_a = passed_back(both[:SHIFT, SHIFT:, a_z], gx)
    came_y = passed_back(both[:, :SHIFT], gy)
    came_ay = passed_back(came_y[:SHIFT, :, a_z], gx)
    both = jnp.concatenate([both[:, SHIFT:], came_y], axis=1)
    came_b = passed_back(both[:SHIFT, :, b_z], gx)
    came_z = passed_back(both[SHIFT:, :, :SHIFT], gz)
    came_xz = passed_back_both(both[:SHIFT, :, :SHIFT], gx, gz)
    far = jnp.concatenate([came_a, came_ay], axis=1)
    half_a = jnp.concatenate([both[SHIFT:, :, a_z], far], axis=0)
    half_b = jnp.concatenate(
        [
            jnp.concatenate([both[SHIFT:, :, b_z], came_b], axis=0),
            jnp.concatenate([came_z, came_xz], axis=0),
        ],
        axis=2,
    )

    def is_last(axes):
        at = jnp.int32(0)
        count = 1
        for axis in axes:
            at = at * lax.axis_size(axis) + lax.axis_index(axis)
            count *= lax.axis_size(axis)
        return (at == count - 1).astype(jnp.int32)

    last_x, last_y, last_z = is_last(gx), is_last(gy), is_last(gz)
    weights = (
        norm_gain.reshape(-1, 1),
        norm_bias.reshape(-1, 1),
        qkv_weight.T,
        qkv_weight,
        qkv_bias.reshape(-1, 1),
        proj_weight,
    )
    out_a, grads_a = windows(jnp.stack([last_x, last_y, 0 * last_z]), half_a, weights)
    out_b, grads_b = windows(jnp.stack([last_x, last_y, last_z]), half_b, weights)
    token_grad = jnp.concatenate([out_a, out_b], axis=2)
    total = summed_everywhere(grads_a + grads_b)
    devices = math.prod(lax.axis_size(axis) for axis in gx + gy + gz)
    total = total * float(math.prod(tokens.shape[:3]) * devices) ** (-0.5)
    main = total[:, :MAIN].reshape(-1, LANES)
    parts = [main[width * j : width * (j + 1)] for j in range(6)]
    half = width - LANES
    qkv_grad = jnp.concatenate(parts[:4] + [parts[5][:, :half]], axis=1)
    proj_grad = jnp.concatenate([parts[4], parts[5][:, half:]], axis=1)
    flat = total[:, MAIN : MAIN + 2].reshape(-1)
    at = 8 * LANES
    return (
        token_grad,
        qkv_grad,
        flat[: 3 * width],
        proj_grad,
        flat[at : at + width],
        flat[at + 2 * LANES : at + 2 * LANES + width],
        flat[at + 4 * LANES : at + 4 * LANES + width],
    )


def solution(mesh):
    split = Mesh(mesh.devices.reshape(4, 4, 2, 2, 4), ("zl", "x", "c", "zh", "y"))
    block = P(("zl", "x"), "c", ("zh", "y"), None)
    return jax.shard_map(
        per_device,
        mesh=split,
        in_specs=(block, block, P(), P(), P(), P(), P()),
        out_specs=(block, P(), P(), P(), P(), P(), P()),
        check_vma=False,
    )
```

```python
import functools
import math

import jax
import jax.numpy as jnp
from jax import lax
from jax.experimental import pallas as pl
from jax.experimental.pallas import tpu as pltpu
from jax.sharding import Mesh, PartitionSpec as P

HEADS = 6
WIN = 8
SHIFT = 4
FAR = -1e30
LANES = 128
PARTS = 8
MAIN = 144
ROWS = MAIN + 8
BEGIN_AT = 3
FINISH_AT = 2
F32 = jnp.float32
BF16 = jnp.bfloat16


def dot(a, b):
    return jnp.dot(a, b, preferred_element_type=F32)


def dot_rows(a, b):
    return lax.dot_general(a, b, (((1,), (1,)), ((), ())), preferred_element_type=F32)


def dot_cols(a, b):
    return lax.dot_general(a, b, (((0,), (0,)), ((), ())), preferred_element_type=F32)


def window_kernel(
    flags, gain, nbias, w_cols, w_rows, qbias, proj, near, *rest,
):
    far = rest[:-8]
    out, grads, acc_qkv, acc_proj, acc_gain, acc_nb, packed_grad, attended = rest[-8:]
    width = w_rows.shape[0]
    count = WIN**3
    windows_here = near.shape[1] // WIN
    size = width // HEADS
    factor = size**-0.5
    scale = factor * math.log2(math.e)
    place = lax.broadcasted_iota(jnp.int32, (16, count), 1)
    row = lax.broadcasted_iota(jnp.int32, (16, count), 0)
    ones = jnp.ones((16, count), BF16)

    class Window:
        pass

    def begin(at):
        here = Window()
        here.at = at
        lo, hi = at * WIN, (at + 1) * WIN
        pieces, start = [], 0
        for piece in far:
            first, last = max(lo - start, 0), min(hi - start, piece.shape[1])
            if first < last:
                pieces.append(piece[:, first:last])
            start += piece.shape[1]
        arrived = jnp.concatenate(
            [near[:, lo:hi].astype(F32), jnp.concatenate(pieces, axis=1).astype(F32)], axis=0
        ).reshape(count, 2 * width)
        here.upward = arrived[:, :width]
        here.upward_half = here.upward.astype(BF16)
        inputs = arrived[:, LANES:].T[width - LANES :]
        centred = inputs - jnp.mean(inputs, axis=0, keepdims=True)
        here.inverse = lax.rsqrt(jnp.mean(centred * centred, axis=0, keepdims=True) + 1e-5)
        here.normed = centred * here.inverse
        here.hidden = (here.normed * gain[...] + nbias[...]).astype(BF16)
        here.packed = (dot(w_cols[...], here.hidden) + qbias[...]).astype(BF16)
        here.att_grad = dot_rows(proj[...], here.upward_half).astype(BF16)
        last = flags[1] if at == windows_here - 1 else 0
        code = (
            4 * flags[0] * ((place >> 8) & 1)
            + 2 * last * ((place >> 5) & 1)
            + flags[2] * ((place >> 2) & 1)
        )
        same = code == row
        here.query_code = jnp.where(same, 1.0, 0.0).astype(BF16)
        here.key_code = jnp.where(same, 0.0, FAR).astype(BF16)
        attended[at, width:, :] = ones
        return here

    def rows_of(kind, head):
        return slice(kind * width + size * head, kind * width + size * (head + 1))

    def score(here, head):
        return dot_cols(
            jnp.concatenate([here.packed[rows_of(1, head)], here.key_code], axis=0),
            jnp.concatenate([here.packed[rows_of(0, head)], here.query_code], axis=0),
        )

    def weigh(scores):
        peak = jnp.max(scores, axis=0, keepdims=True)
        return jnp.exp2((scores - peak) * scale).astype(BF16)

    def values(here, head):
        return jnp.concatenate([here.packed[rows_of(2, head)], ones], axis=0)

    def attend(here, head, expo):
        mixed = dot(values(here, head), expo)
        recip = 1.0 / mixed[size : size + 1]
        result = mixed[:size] * recip
        attended[here.at, rows_of(0, head), :] = result.astype(BF16)
        scaled = (here.att_grad[rows_of(0, head)].astype(F32) * recip).astype(BF16)
        inner = jnp.sum(scaled.astype(F32) * result, axis=0, keepdims=True)
        high = inner.astype(BF16).astype(F32)
        inner_rows = jnp.where(row == 0, -high, jnp.where(row == 1, high - inner, 0.0))
        return scaled, jnp.concatenate([scaled, inner_rows.astype(BF16)], axis=0)

    def pull_back(here, head, expo, scaled, spread):
        score_grad = expo * spread.astype(BF16)
        query, keyset = here.packed[rows_of(0, head)], here.packed[rows_of(1, head)]
        grad_of = packed_grad.at[here.at]
        grad_of[rows_of(2, head), :] = dot_rows(scaled, expo).astype(BF16)
        grad_of[rows_of(0, head), :] = (dot(keyset, score_grad) * factor).astype(BF16)
        grad_of[rows_of(1, head), :] = (dot_rows(score_grad, query).T * factor).astype(BF16)

    def add(total, value, at):
        total[...] = value if at == 0 else total[...] + value

    def finish(here):
        grad_half = packed_grad[here.at]
        add(
            acc_qkv,
            dot_rows(jnp.concatenate([here.hidden, ones], axis=0), grad_half),
            here.at,
        )
        add(acc_proj, dot(attended[here.at], here.upward_half), here.at)
        hidden_grad = dot(w_rows[...], grad_half)
        add(acc_gain, hidden_grad * here.normed, here.at)
        add(acc_nb, hidden_grad, here.at)
        normed_grad = hidden_grad * gain[...]
        first = jnp.mean(normed_grad, axis=0, keepdims=True)
        second = jnp.mean(normed_grad * here.normed, axis=0, keepdims=True)
        change = here.inverse * (normed_grad - first - here.normed * second)
        out[:, here.at * WIN : (here.at + 1) * WIN] = (
            (here.upward + change.T).reshape(WIN, WIN, WIN, width).astype(BF16)
        )

    heads = [(at, head) for at in range(windows_here) for head in range(HEADS)]
    begun = {0: begin(0)}
    scores, earlier = score(begun[0], 0), None
    for number in range(len(heads) + 1):
        inside = number < len(heads)
        at, head = heads[number] if inside else (windows_here, 0)
        if inside and head == BEGIN_AT and at + 1 < windows_here:
            begun[at + 1] = begin(at + 1)
        spread = None
        if earlier is not None:
            before, prior = begun[earlier[0]], earlier[1]
            spread = dot_cols(values(before, prior), earlier[4])
        following = None
        if number + 1 < len(heads):
            next_at, next_head = heads[number + 1]
            following = score(begun[next_at], next_head)
        expo = weigh(scores) if inside else None
        current = (at, head, expo, *attend(begun[at], head, expo)) if inside else None
        if earlier is not None:
            pull_back(before, prior, earlier[2], earlier[3], spread)
        if head == FINISH_AT and 0 < at < windows_here:
            finish(begun[at - 1])
        scores, earlier = following, current
    finish(begun[windows_here - 1])

    def put(at, value):
        done = 0
        while done < value.shape[0]:
            part, inside = divmod(at + done, MAIN)
            rows = min(value.shape[0] - done, MAIN - inside)
            grads[part, inside : inside + rows, :] = value[done : done + rows]
            done += rows

    def put_small(at, value):
        grads[at // 2, MAIN + at % 2, : value.shape[1]] = value[0]

    def over_tokens(value):
        folded = value[:, :LANES]
        for j in range(1, count // LANES):
            folded = folded + value[:, j * LANES : (j + 1) * LANES]
        return jnp.sum(folded.T, axis=0, keepdims=True)

    qkv = acc_qkv[...]
    prj = acc_proj[...]
    for j in range(4):
        put(width * j, qkv[:width, j * LANES : (j + 1) * LANES])
    put(width * 4, prj[:width, :LANES])
    put(
        width * 5,
        jnp.concatenate([qkv[:width, 4 * LANES :], prj[:width, LANES:]], axis=1),
    )
    grads[:, MAIN:, :] = jnp.zeros_like(grads[:, MAIN:, :])
    for j in range(5):
        put_small(j, qkv[width : width + 1, j * LANES : (j + 1) * LANES])
    small = [prj[width : width + 1], over_tokens(acc_gain[...]), over_tokens(acc_nb[...])]
    for j, value in enumerate(small):
        put_small(8 + 2 * j, value[:, :LANES])
        put_small(9 + 2 * j, value[:, LANES:])


def windows(flags, weights, near, *far):
    depth, width_y, depth_z, wide = near.shape
    depth += far[0].shape[0]
    width = wide // 2
    count = WIN**3
    operands = (*weights, near, *far)
    return pl.pallas_call(
        window_kernel,
        in_specs=[pl.BlockSpec(memory_space=pltpu.SMEM)]
        + [pl.BlockSpec(memory_space=pltpu.VMEM)] * len(operands),
        out_specs=[pl.BlockSpec(memory_space=pltpu.VMEM)] * 2,
        out_shape=[
            jax.ShapeDtypeStruct((depth, width_y, depth_z, width), BF16),
            jax.ShapeDtypeStruct((PARTS, ROWS, LANES), F32),
        ],
        scratch_shapes=[
            pltpu.VMEM((width + 16, 3 * width), F32),
            pltpu.VMEM((width + 16, width), F32),
            pltpu.VMEM((width, count), F32),
            pltpu.VMEM((width, count), F32),
            pltpu.VMEM((width_y // WIN, 3 * width, count), BF16),
            pltpu.VMEM((width_y // WIN, width + 16, count), BF16),
        ],
        compiler_params=pltpu.CompilerParams(vmem_limit_bytes=48 * 2**20),
        cost_estimate=pl.CostEstimate(
            flops=20 * 10**9, transcendentals=4 * 10**6, bytes_accessed=4 * 10**6
        ),
        name="window_grads",
    )(flags, *operands)


def swapped(value, axis, bit):
    axes = (axis,) if isinstance(axis, str) else axis
    count = math.prod(lax.axis_size(name) for name in axes)
    return lax.ppermute(value, axis, [(a, a ^ bit) for a in range(count)])


def coded(value):
    small = value[:, MAIN:]
    high = lax.reduce_precision(small, 8, 7)
    return jnp.concatenate([value[:, :MAIN], high, small - high], axis=1).astype(BF16)


def decoded(value):
    wide = value.astype(F32)
    small = wide[:, MAIN:ROWS] + wide[:, ROWS:]
    return jnp.concatenate([wide[:, :MAIN], small], axis=1)


def halve(value, axis):
    half = value.shape[0] // 2
    upper = lax.axis_index(axis) % 2
    kept = lax.dynamic_slice_in_dim(value, upper * half, half, 0)
    given = lax.dynamic_slice_in_dim(value, (1 - upper) * half, half, 0)
    return kept + decoded(swapped(coded(given), axis, 1))


def quarter(value, axis):
    part = value.shape[0] // 4
    at = lax.axis_index(axis)
    sent = coded(value)
    total = lax.dynamic_slice_in_dim(value, at * part, part, 0)
    for bits in (2, 1, 3):
        given = lax.dynamic_slice_in_dim(sent, (at ^ bits) * part, part, 0)
        total = total + decoded(swapped(given, axis, bits))
    return total


def sum_of_two(value, axes, bit):
    sent = coded(value)
    return decoded(sent) + decoded(swapped(sent, axes, bit))


def sum_of_four(value, axes, first, second):
    sent = coded(value)
    both = swapped(sent, axes, first ^ second)
    one, two = swapped(sent, axes, first), swapped(sent, axes, second)
    return (decoded(sent) + decoded(one)) + (decoded(two) + decoded(both))


def join_four(value, axis):
    at = lax.axis_index(axis)
    odd, upper = at % 2 == 1, at >= 2
    far, one, three = (swapped(value, axis, bits) for bits in (2, 1, 3))
    flat = [
        jnp.where(odd, one, value),
        jnp.where(odd, value, one),
        jnp.where(odd, three, far),
        jnp.where(odd, far, three),
    ]
    return jnp.concatenate([jnp.where(upper, flat[j ^ 2], flat[j]) for j in range(4)], axis=0)


def summed_everywhere(value):
    value = quarter(halve(value, "c"), "y")
    value = sum_of_four(value, ("x",), 1, 2)
    value = sum_of_two(value, ("zl", "zh"), 2)
    value = sum_of_four(value, ("zl", "zh"), 4, 1)
    return join_four(coded(value), "y")


def unpack_kernel(upper, mine, other, qkv, proj, qbias, pbias, gain, nbias, *, width, factor):
    here = upper[0] == 1
    first = decoded(jnp.where(here, other[...], mine[...])) * factor
    second = decoded(jnp.where(here, mine[...], other[...])) * factor
    both = jnp.concatenate([first, second], axis=0)
    main = both[:, :MAIN].reshape(PARTS * MAIN, LANES)
    block = lambda j: main[width * j : width * (j + 1)]
    for j in range(4):
        qkv[:, j * LANES : (j + 1) * LANES] = block(j)
    rest = block(5)
    qkv[:, 4 * LANES :] = rest[:, : width - LANES]
    proj[:, :LANES] = block(4)
    proj[:, LANES:] = rest[:, width - LANES :]

    def put(target, at):
        for j in range(-(-target.shape[0] // LANES)):
            wide = min(LANES, target.shape[0] - j * LANES)
            line = both[(at + j) // 2, MAIN + (at + j) % 2]
            target[j * LANES : j * LANES + wide] = line[:wide]

    for target, at in ((qbias, 0), (pbias, 8), (gain, 10), (nbias, 12)):
        put(target, at)


def unpacked(value, axis, width, factor):
    shapes = [(width, 3 * width), (width, width), (3 * width,), (width,), (width,), (width,)]
    return pl.pallas_call(
        functools.partial(unpack_kernel, width=width, factor=factor),
        in_specs=[pl.BlockSpec(memory_space=pltpu.SMEM)]
        + [pl.BlockSpec(memory_space=pltpu.VMEM)] * 2,
        out_specs=[pl.BlockSpec(memory_space=pltpu.VMEM)] * 6,
        out_shape=[jax.ShapeDtypeStruct(shape, F32) for shape in shapes],
        compiler_params=pltpu.CompilerParams(vmem_limit_bytes=16 * 2**20),
        name="unpack_sums",
    )(lax.axis_index(axis).reshape(1), value, swapped(value, axis, 1))


def passed_back(value, axes):
    sizes = [lax.axis_size(axis) for axis in axes]
    count = math.prod(sizes)
    return lax.ppermute(value, axes, [(a, (a - 1) % count) for a in range(count)])


def passed_back_both(value, first, second):
    ones = [lax.axis_size(axis) for axis in first]
    twos = [lax.axis_size(axis) for axis in second]
    n, m = math.prod(ones), math.prod(twos)
    pairs = [
        (a * m + b, ((a - 1) % n) * m + (b - 1) % m) for a in range(n) for b in range(m)
    ]
    return lax.ppermute(value, first + second, pairs)


def per_device(tokens, upstream, norm_gain, norm_bias, qkv_weight, qkv_bias, proj_weight):
    gx, gy, gz = ("zl", "x"), ("c",), ("zh", "y")
    width = tokens.shape[3]
    both = jnp.concatenate([upstream, tokens], axis=3)
    a_z, b_z = slice(SHIFT, SHIFT + WIN), slice(SHIFT + WIN, None)
    came_a = passed_back(both[:SHIFT, SHIFT:, a_z], gx)
    came_y = passed_back(both[:, :SHIFT], gy)
    came_ay = passed_back(came_y[:SHIFT, :, a_z], gx)
    both = jnp.concatenate([both[:, SHIFT:], came_y], axis=1)
    came_b = passed_back(both[:SHIFT, :, b_z], gx)
    came_z = passed_back(both[SHIFT:, :, :SHIFT], gz)
    came_xz = passed_back_both(both[:SHIFT, :, :SHIFT], gx, gz)
    def is_last(axes):
        at = jnp.int32(0)
        count = 1
        for axis in axes:
            at = at * lax.axis_size(axis) + lax.axis_index(axis)
            count *= lax.axis_size(axis)
        return (at == count - 1).astype(jnp.int32)

    last_x, last_y, last_z = is_last(gx), is_last(gy), is_last(gz)
    weights = (
        norm_gain.reshape(-1, 1),
        norm_bias.reshape(-1, 1),
        qkv_weight.T,
        qkv_weight,
        qkv_bias.reshape(-1, 1),
        proj_weight,
    )
    out_a, grads_a = windows(
        jnp.stack([last_x, last_y, 0 * last_z]), weights, both[SHIFT:, :, a_z], came_a, came_ay
    )
    out_b, grads_b = windows(
        jnp.stack([last_x, last_y, last_z]),
        weights,
        jnp.concatenate([both[SHIFT:, :, b_z], came_z], axis=2),
        jnp.concatenate([came_b, came_xz], axis=2),
    )
    token_grad = jnp.concatenate([out_a, out_b], axis=2)
    devices = math.prod(lax.axis_size(axis) for axis in gx + gy + gz)
    factor = float(math.prod(tokens.shape[:3]) * devices) ** (-0.5)
    quarters = summed_everywhere(grads_a + grads_b)
    qkv_grad, proj_grad, qbias_grad, pbias_grad, gain_grad, nbias_grad = unpacked(
        quarters, "c", width, factor
    )
    return (token_grad, qkv_grad, qbias_grad, proj_grad, pbias_grad, gain_grad, nbias_grad)


def solution(mesh):
    split = Mesh(mesh.devices.reshape(4, 4, 2, 2, 4), ("zl", "x", "c", "zh", "y"))
    block = P(("zl", "x"), "c", ("zh", "y"), None)
    return jax.shard_map(
        per_device,
        mesh=split,
        in_specs=(block, block, P(), P(), P(), P(), P()),
        out_specs=(block, P(), P(), P(), P(), P(), P()),
        check_vma=False,
    )
```

```python
import functools
import math

import jax
import jax.numpy as jnp
from jax import lax
from jax.experimental import pallas as pl
from jax.experimental.pallas import tpu as pltpu
from jax.sharding import Mesh, PartitionSpec as P

HEADS = 6
WIN = 8
SHIFT = 4
FAR = -1e30
LANES = 128
PARTS = 8
MAIN = 144
ROWS = MAIN + 8
BEGIN_AT = 3
FINISH_AT = 2
F32 = jnp.float32
BF16 = jnp.bfloat16


def dot(a, b):
    return jnp.dot(a, b, preferred_element_type=F32)


def dot_rows(a, b):
    return lax.dot_general(a, b, (((1,), (1,)), ((), ())), preferred_element_type=F32)


def dot_cols(a, b):
    return lax.dot_general(a, b, (((0,), (0,)), ((), ())), preferred_element_type=F32)


def window_kernel(
    flags, gain, nbias, w_cols, w_rows, qbias, proj, near, *rest,
):
    far = rest[:-8]
    out, grads, acc_qkv, acc_proj, acc_gain, acc_nb, packed_grad, attended = rest[-8:]
    width = w_rows.shape[0]
    count = WIN**3
    windows_here = near.shape[1] // WIN
    size = width // HEADS
    factor = size**-0.5
    scale = factor * math.log2(math.e)
    place = lax.broadcasted_iota(jnp.int32, (16, count), 1)
    row = lax.broadcasted_iota(jnp.int32, (16, count), 0)
    ones = jnp.ones((16, count), BF16)

    class Window:
        pass

    def begin(at):
        here = Window()
        here.at = at
        lo, hi = at * WIN, (at + 1) * WIN
        pieces, start = [], 0
        for piece in far:
            first, last = max(lo - start, 0), min(hi - start, piece.shape[1])
            if first < last:
                pieces.append(piece[:, first:last])
            start += piece.shape[1]
        arrived = jnp.concatenate(
            [near[:, lo:hi].astype(F32), jnp.concatenate(pieces, axis=1).astype(F32)], axis=0
        ).reshape(count, 2 * width)
        here.upward = arrived[:, :width]
        here.upward_half = here.upward.astype(BF16)
        inputs = arrived[:, LANES:].T[width - LANES :]
        centred = inputs - jnp.mean(inputs, axis=0, keepdims=True)
        here.inverse = lax.rsqrt(jnp.mean(centred * centred, axis=0, keepdims=True) + 1e-5)
        here.normed = centred * here.inverse
        here.hidden = (here.normed * gain[...] + nbias[...]).astype(BF16)
        here.packed = (dot(w_cols[...], here.hidden) + qbias[...]).astype(BF16)
        here.att_grad = dot_rows(proj[...], here.upward_half).astype(BF16)
        last = flags[1] if at == windows_here - 1 else 0
        code = (
            4 * flags[0] * ((place >> 8) & 1)
            + 2 * last * ((place >> 5) & 1)
            + flags[2] * ((place >> 2) & 1)
        )
        same = code == row
        here.query_code = jnp.where(same, 1.0, 0.0).astype(BF16)
        here.key_code = jnp.where(same, 0.0, FAR).astype(BF16)
        attended[at, width:, :] = ones
        return here

    def rows_of(kind, head):
        return slice(kind * width + size * head, kind * width + size * (head + 1))

    def score(here, head):
        return dot_cols(
            jnp.concatenate([here.packed[rows_of(1, head)], here.key_code], axis=0),
            jnp.concatenate([here.packed[rows_of(0, head)], here.query_code], axis=0),
        )

    def weigh(scores):
        peak = jnp.max(scores, axis=0, keepdims=True)
        return jnp.exp2((scores - peak) * scale).astype(BF16)

    def values(here, head):
        return jnp.concatenate([here.packed[rows_of(2, head)], ones], axis=0)

    def attend(here, head, expo):
        mixed = dot(values(here, head), expo)
        recip = 1.0 / mixed[size : size + 1]
        result = mixed[:size] * recip
        attended[here.at, rows_of(0, head), :] = result.astype(BF16)
        scaled = (here.att_grad[rows_of(0, head)].astype(F32) * recip).astype(BF16)
        inner = jnp.sum(scaled.astype(F32) * result, axis=0, keepdims=True)
        high = inner.astype(BF16).astype(F32)
        inner_rows = jnp.where(row == 0, -high, jnp.where(row == 1, high - inner, 0.0))
        return scaled, jnp.concatenate([scaled, inner_rows.astype(BF16)], axis=0)

    def pull_back(here, head, expo, scaled, spread):
        score_grad = expo * spread.astype(BF16)
        query, keyset = here.packed[rows_of(0, head)], here.packed[rows_of(1, head)]
        grad_of = packed_grad.at[here.at]
        grad_of[rows_of(2, head), :] = dot_rows(scaled, expo).astype(BF16)
        grad_of[rows_of(0, head), :] = (dot(keyset, score_grad) * factor).astype(BF16)
        grad_of[rows_of(1, head), :] = (dot_rows(score_grad, query).T * factor).astype(BF16)

    def add(total, value, at):
        total[...] = value if at == 0 else total[...] + value

    def finish(here):
        grad_half = packed_grad[here.at]
        add(
            acc_qkv,
            dot_rows(jnp.concatenate([here.hidden, ones], axis=0), grad_half),
            here.at,
        )
        add(acc_proj, dot(attended[here.at], here.upward_half), here.at)
        hidden_grad = dot(w_rows[...], grad_half)
        add(acc_gain, hidden_grad * here.normed, here.at)
        add(acc_nb, hidden_grad, here.at)
        normed_grad = hidden_grad * gain[...]
        first = jnp.mean(normed_grad, axis=0, keepdims=True)
        second = jnp.mean(normed_grad * here.normed, axis=0, keepdims=True)
        change = here.inverse * (normed_grad - first - here.normed * second)
        out[:, here.at * WIN : (here.at + 1) * WIN] = (
            (here.upward + change.T).reshape(WIN, WIN, WIN, width).astype(BF16)
        )

    heads = [(at, head) for at in range(windows_here) for head in range(HEADS)]
    begun = {0: begin(0)}
    scores, earlier = score(begun[0], 0), None
    for number in range(len(heads) + 1):
        inside = number < len(heads)
        at, head = heads[number] if inside else (windows_here, 0)
        if inside and head == BEGIN_AT and at + 1 < windows_here:
            begun[at + 1] = begin(at + 1)
        spread = None
        if earlier is not None:
            before, prior = begun[earlier[0]], earlier[1]
            spread = dot_cols(values(before, prior), earlier[4])
        following = None
        if number + 1 < len(heads):
            next_at, next_head = heads[number + 1]
            following = score(begun[next_at], next_head)
        expo = weigh(scores) if inside else None
        current = (at, head, expo, *attend(begun[at], head, expo)) if inside else None
        if earlier is not None:
            pull_back(before, prior, earlier[2], earlier[3], spread)
        if head == FINISH_AT and 0 < at < windows_here:
            finish(begun[at - 1])
        scores, earlier = following, current
    finish(begun[windows_here - 1])

    def put(at, value):
        done = 0
        while done < value.shape[0]:
            part, inside = divmod(at + done, MAIN)
            rows = min(value.shape[0] - done, MAIN - inside)
            grads[part, inside : inside + rows, :] = value[done : done + rows]
            done += rows

    def put_small(at, value):
        grads[at // 2, MAIN + at % 2, : value.shape[1]] = value[0]

    def over_tokens(value):
        folded = value[:, :LANES]
        for j in range(1, count // LANES):
            folded = folded + value[:, j * LANES : (j + 1) * LANES]
        return jnp.sum(folded.T, axis=0, keepdims=True)

    qkv = acc_qkv[...]
    prj = acc_proj[...]
    for j in range(4):
        put(width * j, qkv[:width, j * LANES : (j + 1) * LANES])
    put(width * 4, prj[:width, :LANES])
    put(
        width * 5,
        jnp.concatenate([qkv[:width, 4 * LANES :], prj[:width, LANES:]], axis=1),
    )
    grads[:, MAIN:, :] = jnp.zeros_like(grads[:, MAIN:, :])
    for j in range(5):
        put_small(j, qkv[width : width + 1, j * LANES : (j + 1) * LANES])
    small = [prj[width : width + 1], over_tokens(acc_gain[...]), over_tokens(acc_nb[...])]
    for j, value in enumerate(small):
        put_small(8 + 2 * j, value[:, :LANES])
        put_small(9 + 2 * j, value[:, LANES:])


def windows(flags, weights, near, *far):
    depth, width_y, depth_z, wide = near.shape
    depth += far[0].shape[0]
    width = wide // 2
    count = WIN**3
    operands = (*weights, near, *far)
    return pl.pallas_call(
        window_kernel,
        in_specs=[pl.BlockSpec(memory_space=pltpu.SMEM)]
        + [pl.BlockSpec(memory_space=pltpu.VMEM)] * len(operands),
        out_specs=[pl.BlockSpec(memory_space=pltpu.VMEM)] * 2,
        out_shape=[
            jax.ShapeDtypeStruct((depth, width_y, depth_z, width), BF16),
            jax.ShapeDtypeStruct((PARTS, ROWS, LANES), F32),
        ],
        scratch_shapes=[
            pltpu.VMEM((width + 16, 3 * width), F32),
            pltpu.VMEM((width + 16, width), F32),
            pltpu.VMEM((width, count), F32),
            pltpu.VMEM((width, count), F32),
            pltpu.VMEM((width_y // WIN, 3 * width, count), BF16),
            pltpu.VMEM((width_y // WIN, width + 16, count), BF16),
        ],
        compiler_params=pltpu.CompilerParams(vmem_limit_bytes=48 * 2**20),
        cost_estimate=pl.CostEstimate(
            flops=20 * 10**9, transcendentals=4 * 10**6, bytes_accessed=4 * 10**6
        ),
        name="window_grads",
    )(flags, *operands)


def swapped(value, axis, bit):
    axes = (axis,) if isinstance(axis, str) else axis
    count = math.prod(lax.axis_size(name) for name in axes)
    return lax.ppermute(value, axis, [(a, a ^ bit) for a in range(count)])


def coded(value):
    small = value[:, MAIN:]
    high = lax.reduce_precision(small, 8, 7)
    return jnp.concatenate([value[:, :MAIN], high, small - high], axis=1).astype(BF16)


def decoded(value):
    wide = value.astype(F32)
    small = wide[:, MAIN:ROWS] + wide[:, ROWS:]
    return jnp.concatenate([wide[:, :MAIN], small], axis=1)


def halve(value, axis):
    half = value.shape[0] // 2
    upper = lax.axis_index(axis) % 2
    kept = lax.dynamic_slice_in_dim(value, upper * half, half, 0)
    given = lax.dynamic_slice_in_dim(value, (1 - upper) * half, half, 0)
    return kept + decoded(swapped(coded(given), axis, 1))


def quarter(value, axis):
    part = value.shape[0] // 4
    at = lax.axis_index(axis)
    sent = coded(value)
    total = lax.dynamic_slice_in_dim(value, at * part, part, 0)
    for bits in (2, 1, 3):
        given = lax.dynamic_slice_in_dim(sent, (at ^ bits) * part, part, 0)
        total = total + decoded(swapped(given, axis, bits))
    return total


def sum_of_two(value, axes, bit):
    sent = coded(value)
    return decoded(sent) + decoded(swapped(sent, axes, bit))


def sum_of_four(value, axes, first, second):
    sent = coded(value)
    both = swapped(sent, axes, first ^ second)
    one, two = swapped(sent, axes, first), swapped(sent, axes, second)
    return (decoded(sent) + decoded(one)) + (decoded(two) + decoded(both))


def join(value, axis):
    upper = lax.axis_index(axis) % 2 == 1
    other = swapped(value, axis, 1)
    return jnp.concatenate(
        [jnp.where(upper, other, value), jnp.where(upper, value, other)], axis=0
    )


def join_four(value, axis):
    at = lax.axis_index(axis)
    odd, upper = at % 2 == 1, at >= 2
    far, one, three = (swapped(value, axis, bits) for bits in (2, 1, 3))
    flat = [
        jnp.where(odd, one, value),
        jnp.where(odd, value, one),
        jnp.where(odd, three, far),
        jnp.where(odd, far, three),
    ]
    return jnp.concatenate([jnp.where(upper, flat[j ^ 2], flat[j]) for j in range(4)], axis=0)


def summed_everywhere(value):
    value = quarter(halve(value, "c"), "y")
    value = sum_of_four(value, ("x",), 1, 2)
    value = sum_of_two(value, ("zl", "zh"), 2)
    value = sum_of_four(value, ("zl", "zh"), 4, 1)
    return decoded(join(join_four(coded(value), "y"), "c"))


def passed_back(value, axes):
    sizes = [lax.axis_size(axis) for axis in axes]
    count = math.prod(sizes)
    return lax.ppermute(value, axes, [(a, (a - 1) % count) for a in range(count)])


def passed_back_both(value, first, second):
    ones = [lax.axis_size(axis) for axis in first]
    twos = [lax.axis_size(axis) for axis in second]
    n, m = math.prod(ones), math.prod(twos)
    pairs = [
        (a * m + b, ((a - 1) % n) * m + (b - 1) % m) for a in range(n) for b in range(m)
    ]
    return lax.ppermute(value, first + second, pairs)


def per_device(tokens, upstream, norm_gain, norm_bias, qkv_weight, qkv_bias, proj_weight):
    gx, gy, gz = ("zl", "x"), ("c",), ("zh", "y")
    width = tokens.shape[3]
    both = jnp.concatenate([upstream, tokens], axis=3)
    a_z, b_z = slice(SHIFT, SHIFT + WIN), slice(SHIFT + WIN, None)
    came_a = passed_back(both[:SHIFT, SHIFT:, a_z], gx)
    came_y = passed_back(both[:, :SHIFT], gy)
    came_ay = passed_back(came_y[:SHIFT, :, a_z], gx)
    both = jnp.concatenate([both[:, SHIFT:], came_y], axis=1)
    came_b = passed_back(both[:SHIFT, :, b_z], gx)
    came_z = passed_back(both[SHIFT:, :, :SHIFT], gz)
    came_xz = passed_back_both(both[:SHIFT, :, :SHIFT], gx, gz)
    def is_last(axes):
        at = jnp.int32(0)
        count = 1
        for axis in axes:
            at = at * lax.axis_size(axis) + lax.axis_index(axis)
            count *= lax.axis_size(axis)
        return (at == count - 1).astype(jnp.int32)

    last_x, last_y, last_z = is_last(gx), is_last(gy), is_last(gz)
    weights = (
        norm_gain.reshape(-1, 1),
        norm_bias.reshape(-1, 1),
        qkv_weight.T,
        qkv_weight,
        qkv_bias.reshape(-1, 1),
        proj_weight,
    )
    out_a, grads_a = windows(
        jnp.stack([last_x, last_y, 0 * last_z]), weights, both[SHIFT:, :, a_z], came_a, came_ay
    )
    out_b, grads_b = windows(
        jnp.stack([last_x, last_y, last_z]),
        weights,
        jnp.concatenate([both[SHIFT:, :, b_z], came_z], axis=2),
        jnp.concatenate([came_b, came_xz], axis=2),
    )
    token_grad = jnp.concatenate([out_a, out_b], axis=2)
    total = summed_everywhere(grads_a + grads_b)
    devices = math.prod(lax.axis_size(axis) for axis in gx + gy + gz)
    total = total * float(math.prod(tokens.shape[:3]) * devices) ** (-0.5)
    main = total[:, :MAIN].reshape(-1, LANES)
    parts = [main[width * j : width * (j + 1)] for j in range(6)]
    half = width - LANES
    qkv_grad = jnp.concatenate(parts[:4] + [parts[5][:, :half]], axis=1)
    proj_grad = jnp.concatenate([parts[4], parts[5][:, half:]], axis=1)
    flat = total[:, MAIN : MAIN + 2].reshape(-1)
    at = 8 * LANES
    return (
        token_grad,
        qkv_grad,
        flat[: 3 * width],
        proj_grad,
        flat[at : at + width],
        flat[at + 2 * LANES : at + 2 * LANES + width],
        flat[at + 4 * LANES : at + 4 * LANES + width],
    )


def solution(mesh):
    split = Mesh(mesh.devices.reshape(4, 4, 2, 2, 4), ("zl", "x", "c", "zh", "y"))
    block = P(("zl", "x"), "c", ("zh", "y"), None)
    return jax.shard_map(
        per_device,
        mesh=split,
        in_specs=(block, block, P(), P(), P(), P(), P()),
        out_specs=(block, P(), P(), P(), P(), P(), P()),
        check_vma=False,
    )
```

```python
import functools
import math

import jax
import jax.numpy as jnp
from jax import lax
from jax.experimental import pallas as pl
from jax.experimental.pallas import tpu as pltpu
from jax.sharding import Mesh, PartitionSpec as P

HEADS = 6
WIN = 8
SHIFT = 4
FAR = -1e30
LANES = 128
PARTS = 8
MAIN = 144
ROWS = MAIN + 8
BEGIN_AT = 3
STEPS_A = 1
STEPS_B = 2
FINISH_AT = 2
F32 = jnp.float32
BF16 = jnp.bfloat16


def dot(a, b):
    return jnp.dot(a, b, preferred_element_type=F32)


def dot_rows(a, b):
    return lax.dot_general(a, b, (((1,), (1,)), ((), ())), preferred_element_type=F32)


def dot_cols(a, b):
    return lax.dot_general(a, b, (((0,), (0,)), ((), ())), preferred_element_type=F32)


def window_kernel(
    flags, gain, nbias, w_cols, w_rows, qbias, proj, near, *rest, steps
):
    far = rest[:-8]
    out, grads, acc_qkv, acc_proj, acc_gain, acc_nb, packed_grad, attended = rest[-8:]
    width = w_rows.shape[0]
    count = WIN**3
    windows_here = near.shape[1] // WIN // steps
    step = pl.program_id(0)
    size = width // HEADS
    factor = size**-0.5
    scale = factor * math.log2(math.e)
    place = lax.broadcasted_iota(jnp.int32, (16, count), 1)
    row = lax.broadcasted_iota(jnp.int32, (16, count), 0)
    ones = jnp.ones((16, count), BF16)

    class Window:
        pass

    def begin(at):
        here = Window()
        here.at = at
        def gathered(lo, hi):
            pieces, start = [], 0
            for piece in far:
                first, last = max(lo - start, 0), min(hi - start, piece.shape[1])
                if first < last:
                    pieces.append(piece[:, first:last].astype(F32))
                start += piece.shape[1]
            return jnp.concatenate(pieces, axis=1)

        wide = windows_here * WIN
        received = gathered(at * WIN, (at + 1) * WIN)
        for j in range(1, steps):
            other = gathered(j * wide + at * WIN, j * wide + (at + 1) * WIN)
            received = jnp.where(step == j, other, received)
        own = near[:, pl.ds(step * wide + at * WIN, WIN)].astype(F32)
        arrived = jnp.concatenate([own, received], axis=0).reshape(count, 2 * width)
        here.upward = arrived[:, :width]
        here.upward_half = here.upward.astype(BF16)
        inputs = arrived[:, LANES:].T[width - LANES :]
        centred = inputs - jnp.mean(inputs, axis=0, keepdims=True)
        here.inverse = lax.rsqrt(jnp.mean(centred * centred, axis=0, keepdims=True) + 1e-5)
        here.normed = centred * here.inverse
        here.hidden = (here.normed * gain[...] + nbias[...]).astype(BF16)
        here.packed = (dot(w_cols[...], here.hidden) + qbias[...]).astype(BF16)
        here.att_grad = dot_rows(proj[...], here.upward_half).astype(BF16)
        last = jnp.where(step == steps - 1, flags[1], 0) if at == windows_here - 1 else 0
        code = (
            4 * flags[0] * ((place >> 8) & 1)
            + 2 * last * ((place >> 5) & 1)
            + flags[2] * ((place >> 2) & 1)
        )
        same = code == row
        here.query_code = jnp.where(same, 1.0, 0.0).astype(BF16)
        here.key_code = jnp.where(same, 0.0, FAR).astype(BF16)
        attended[at, width:, :] = ones
        return here

    def rows_of(kind, head):
        return slice(kind * width + size * head, kind * width + size * (head + 1))

    def score(here, head):
        return dot_cols(
            jnp.concatenate([here.packed[rows_of(1, head)], here.key_code], axis=0),
            jnp.concatenate([here.packed[rows_of(0, head)], here.query_code], axis=0),
        )

    def weigh(scores):
        peak = jnp.max(scores, axis=0, keepdims=True)
        return jnp.exp2((scores - peak) * scale).astype(BF16)

    def values(here, head):
        return jnp.concatenate([here.packed[rows_of(2, head)], ones], axis=0)

    def attend(here, head, expo):
        mixed = dot(values(here, head), expo)
        recip = 1.0 / mixed[size : size + 1]
        result = mixed[:size] * recip
        attended[here.at, rows_of(0, head), :] = result.astype(BF16)
        scaled = (here.att_grad[rows_of(0, head)].astype(F32) * recip).astype(BF16)
        inner = jnp.sum(scaled.astype(F32) * result, axis=0, keepdims=True)
        high = inner.astype(BF16).astype(F32)
        inner_rows = jnp.where(row == 0, -high, jnp.where(row == 1, high - inner, 0.0))
        return scaled, jnp.concatenate([scaled, inner_rows.astype(BF16)], axis=0)

    def pull_back(here, head, expo, scaled, spread):
        score_grad = expo * spread.astype(BF16)
        query, keyset = here.packed[rows_of(0, head)], here.packed[rows_of(1, head)]
        grad_of = packed_grad.at[here.at]
        grad_of[rows_of(2, head), :] = dot_rows(scaled, expo).astype(BF16)
        grad_of[rows_of(0, head), :] = (dot(keyset, score_grad) * factor).astype(BF16)
        grad_of[rows_of(1, head), :] = (dot_rows(score_grad, query).T * factor).astype(BF16)

    def add(total, value, at):
        if at == 0:
            value = jnp.where(step == 0, 0.0, total[...]) + value if steps > 1 else value
            total[...] = value
        else:
            total[...] = total[...] + value

    def finish(here):
        grad_half = packed_grad[here.at]
        add(
            acc_qkv,
            dot_rows(jnp.concatenate([here.hidden, ones], axis=0), grad_half),
            here.at,
        )
        add(acc_proj, dot(attended[here.at], here.upward_half), here.at)
        hidden_grad = dot(w_rows[...], grad_half)
        add(acc_gain, hidden_grad * here.normed, here.at)
        add(acc_nb, hidden_grad, here.at)
        normed_grad = hidden_grad * gain[...]
        first = jnp.mean(normed_grad, axis=0, keepdims=True)
        second = jnp.mean(normed_grad * here.normed, axis=0, keepdims=True)
        change = here.inverse * (normed_grad - first - here.normed * second)
        out[:, here.at * WIN : (here.at + 1) * WIN] = (
            (here.upward + change.T).reshape(WIN, WIN, WIN, width).astype(BF16)
        )

    heads = [(at, head) for at in range(windows_here) for head in range(HEADS)]
    begun = {0: begin(0)}
    scores, earlier = score(begun[0], 0), None
    for number in range(len(heads) + 1):
        inside = number < len(heads)
        at, head = heads[number] if inside else (windows_here, 0)
        if inside and head == BEGIN_AT and at + 1 < windows_here:
            begun[at + 1] = begin(at + 1)
        spread = None
        if earlier is not None:
            before, prior = begun[earlier[0]], earlier[1]
            spread = dot_cols(values(before, prior), earlier[4])
        following = None
        if number + 1 < len(heads):
            next_at, next_head = heads[number + 1]
            following = score(begun[next_at], next_head)
        expo = weigh(scores) if inside else None
        current = (at, head, expo, *attend(begun[at], head, expo)) if inside else None
        if earlier is not None:
            pull_back(before, prior, earlier[2], earlier[3], spread)
        if head == FINISH_AT and 0 < at < windows_here:
            finish(begun[at - 1])
        scores, earlier = following, current
    finish(begun[windows_here - 1])

    def put(at, value):
        done = 0
        while done < value.shape[0]:
            part, inside = divmod(at + done, MAIN)
            rows = min(value.shape[0] - done, MAIN - inside)
            grads[part, inside : inside + rows, :] = value[done : done + rows]
            done += rows

    def put_small(at, value):
        grads[at // 2, MAIN + at % 2, : value.shape[1]] = value[0]

    def over_tokens(value):
        folded = value[:, :LANES]
        for j in range(1, count // LANES):
            folded = folded + value[:, j * LANES : (j + 1) * LANES]
        return jnp.sum(folded.T, axis=0, keepdims=True)

    qkv = acc_qkv[...]
    prj = acc_proj[...]
    for j in range(4):
        put(width * j, qkv[:width, j * LANES : (j + 1) * LANES])
    put(width * 4, prj[:width, :LANES])
    put(
        width * 5,
        jnp.concatenate([qkv[:width, 4 * LANES :], prj[:width, LANES:]], axis=1),
    )
    grads[:, MAIN:, :] = jnp.zeros_like(grads[:, MAIN:, :])
    for j in range(5):
        put_small(j, qkv[width : width + 1, j * LANES : (j + 1) * LANES])
    small = [prj[width : width + 1], over_tokens(acc_gain[...]), over_tokens(acc_nb[...])]
    for j, value in enumerate(small):
        put_small(8 + 2 * j, value[:, :LANES])
        put_small(9 + 2 * j, value[:, LANES:])


def windows(steps, flags, weights, near, *far):
    depth, width_y, depth_z, wide = near.shape
    depth += far[0].shape[0]
    width = wide // 2
    count = WIN**3
    operands = (*weights, near, *far)
    return pl.pallas_call(
        functools.partial(window_kernel, steps=steps),
        grid=(steps,),
        in_specs=[pl.BlockSpec(memory_space=pltpu.SMEM)]
        + [pl.BlockSpec(memory_space=pltpu.VMEM)] * len(operands),
        out_specs=[
            pl.BlockSpec((depth, width_y // steps, depth_z, width), lambda i: (0, i, 0, 0)),
            pl.BlockSpec((PARTS, ROWS, LANES), lambda i: (0, 0, 0)),
        ],
        out_shape=[
            jax.ShapeDtypeStruct((depth, width_y, depth_z, width), BF16),
            jax.ShapeDtypeStruct((PARTS, ROWS, LANES), F32),
        ],
        scratch_shapes=[
            pltpu.VMEM((width + 16, 3 * width), F32),
            pltpu.VMEM((width + 16, width), F32),
            pltpu.VMEM((width, count), F32),
            pltpu.VMEM((width, count), F32),
            pltpu.VMEM((width_y // WIN // steps, 3 * width, count), BF16),
            pltpu.VMEM((width_y // WIN // steps, width + 16, count), BF16),
        ],
        compiler_params=pltpu.CompilerParams(vmem_limit_bytes=48 * 2**20),
        cost_estimate=pl.CostEstimate(
            flops=20 * 10**9, transcendentals=4 * 10**6, bytes_accessed=4 * 10**6
        ),
        name="window_grads",
    )(flags, *operands)


def swapped(value, axis, bit):
    axes = (axis,) if isinstance(axis, str) else axis
    count = math.prod(lax.axis_size(name) for name in axes)
    return lax.ppermute(value, axis, [(a, a ^ bit) for a in range(count)])


def coded(value):
    small = value[:, MAIN:]
    high = lax.reduce_precision(small, 8, 7)
    return jnp.concatenate([value[:, :MAIN], high, small - high], axis=1).astype(BF16)


def decoded(value):
    wide = value.astype(F32)
    small = wide[:, MAIN:ROWS] + wide[:, ROWS:]
    return jnp.concatenate([wide[:, :MAIN], small], axis=1)


def halve(value, axis):
    half = value.shape[0] // 2
    upper = lax.axis_index(axis) % 2
    kept = lax.dynamic_slice_in_dim(value, upper * half, half, 0)
    given = lax.dynamic_slice_in_dim(value, (1 - upper) * half, half, 0)
    return kept + decoded(swapped(coded(given), axis, 1))


def quarter(value, axis):
    part = value.shape[0] // 4
    at = lax.axis_index(axis)
    sent = coded(value)
    total = lax.dynamic_slice_in_dim(value, at * part, part, 0)
    for bits in (2, 1, 3):
        given = lax.dynamic_slice_in_dim(sent, (at ^ bits) * part, part, 0)
        total = total + decoded(swapped(given, axis, bits))
    return total


def sum_of_two(value, axes, bit):
    sent = coded(value)
    return decoded(sent) + decoded(swapped(sent, axes, bit))


def sum_of_four(value, axes, first, second):
    sent = coded(value)
    both = swapped(sent, axes, first ^ second)
    one, two = swapped(sent, axes, first), swapped(sent, axes, second)
    return (decoded(sent) + decoded(one)) + (decoded(two) + decoded(both))


def join_four(value, axis):
    at = lax.axis_index(axis)
    odd, upper = at % 2 == 1, at >= 2
    far, one, three = (swapped(value, axis, bits) for bits in (2, 1, 3))
    flat = [
        jnp.where(odd, one, value),
        jnp.where(odd, value, one),
        jnp.where(odd, three, far),
        jnp.where(odd, far, three),
    ]
    return jnp.concatenate([jnp.where(upper, flat[j ^ 2], flat[j]) for j in range(4)], axis=0)


def summed_everywhere(value):
    value = quarter(halve(value, "c"), "y")
    value = sum_of_four(value, ("x",), 1, 2)
    value = sum_of_two(value, ("zl", "zh"), 2)
    value = sum_of_four(value, ("zl", "zh"), 4, 1)
    return join_four(coded(value), "y")


def unpack_kernel(upper, mine, other, qkv, proj, qbias, pbias, gain, nbias, *, width, factor):
    here = upper[0] == 1
    first = decoded(jnp.where(here, other[...], mine[...])) * factor
    second = decoded(jnp.where(here, mine[...], other[...])) * factor
    both = jnp.concatenate([first, second], axis=0)
    main = both[:, :MAIN].reshape(PARTS * MAIN, LANES)
    block = lambda j: main[width * j : width * (j + 1)]
    for j in range(4):
        qkv[:, j * LANES : (j + 1) * LANES] = block(j)
    rest = block(5)
    qkv[:, 4 * LANES :] = rest[:, : width - LANES]
    proj[:, :LANES] = block(4)
    proj[:, LANES:] = rest[:, width - LANES :]

    def put(target, at):
        for j in range(-(-target.shape[0] // LANES)):
            wide = min(LANES, target.shape[0] - j * LANES)
            line = both[(at + j) // 2, MAIN + (at + j) % 2]
            target[j * LANES : j * LANES + wide] = line[:wide]

    for target, at in ((qbias, 0), (pbias, 8), (gain, 10), (nbias, 12)):
        put(target, at)


def unpacked(value, axis, width, factor):
    shapes = [(width, 3 * width), (width, width), (3 * width,), (width,), (width,), (width,)]
    return pl.pallas_call(
        functools.partial(unpack_kernel, width=width, factor=factor),
        in_specs=[pl.BlockSpec(memory_space=pltpu.SMEM)]
        + [pl.BlockSpec(memory_space=pltpu.VMEM)] * 2,
        out_specs=[pl.BlockSpec(memory_space=pltpu.VMEM)] * 6,
        out_shape=[jax.ShapeDtypeStruct(shape, F32) for shape in shapes],
        compiler_params=pltpu.CompilerParams(vmem_limit_bytes=16 * 2**20),
        name="unpack_sums",
    )(lax.axis_index(axis).reshape(1), value, swapped(value, axis, 1))


def passed_back(value, axes):
    sizes = [lax.axis_size(axis) for axis in axes]
    count = math.prod(sizes)
    return lax.ppermute(value, axes, [(a, (a - 1) % count) for a in range(count)])


def passed_back_both(value, first, second):
    ones = [lax.axis_size(axis) for axis in first]
    twos = [lax.axis_size(axis) for axis in second]
    n, m = math.prod(ones), math.prod(twos)
    pairs = [
        (a * m + b, ((a - 1) % n) * m + (b - 1) % m) for a in range(n) for b in range(m)
    ]
    return lax.ppermute(value, first + second, pairs)


def per_device(tokens, upstream, norm_gain, norm_bias, qkv_weight, qkv_bias, proj_weight):
    gx, gy, gz = ("zl", "x"), ("c",), ("zh", "y")
    width = tokens.shape[3]
    both = jnp.concatenate([upstream, tokens], axis=3)
    a_z, b_z = slice(SHIFT, SHIFT + WIN), slice(SHIFT + WIN, None)
    came_a = passed_back(both[:SHIFT, SHIFT:, a_z], gx)
    came_y = passed_back(both[:, :SHIFT], gy)
    came_ay = passed_back(came_y[:SHIFT, :, a_z], gx)
    both = jnp.concatenate([both[:, SHIFT:], came_y], axis=1)
    came_b = passed_back(both[:SHIFT, :, b_z], gx)
    came_z = passed_back(both[SHIFT:, :, :SHIFT], gz)
    came_xz = passed_back_both(both[:SHIFT, :, :SHIFT], gx, gz)
    def is_last(axes):
        at = jnp.int32(0)
        count = 1
        for axis in axes:
            at = at * lax.axis_size(axis) + lax.axis_index(axis)
            count *= lax.axis_size(axis)
        return (at == count - 1).astype(jnp.int32)

    last_x, last_y, last_z = is_last(gx), is_last(gy), is_last(gz)
    weights = (
        norm_gain.reshape(-1, 1),
        norm_bias.reshape(-1, 1),
        qkv_weight.T,
        qkv_weight,
        qkv_bias.reshape(-1, 1),
        proj_weight,
    )
    out_a, grads_a = windows(
        STEPS_A,
        jnp.stack([last_x, last_y, 0 * last_z]), weights, both[SHIFT:, :, a_z], came_a, came_ay
    )
    out_b, grads_b = windows(
        STEPS_B,
        jnp.stack([last_x, last_y, last_z]),
        weights,
        jnp.concatenate([both[SHIFT:, :, b_z], came_z], axis=2),
        jnp.concatenate([came_b, came_xz], axis=2),
    )
    token_grad = jnp.concatenate([out_a, out_b], axis=2)
    devices = math.prod(lax.axis_size(axis) for axis in gx + gy + gz)
    factor = float(math.prod(tokens.shape[:3]) * devices) ** (-0.5)
    quarters = summed_everywhere(grads_a + grads_b)
    qkv_grad, proj_grad, qbias_grad, pbias_grad, gain_grad, nbias_grad = unpacked(
        quarters, "c", width, factor
    )
    return (token_grad, qkv_grad, qbias_grad, proj_grad, pbias_grad, gain_grad, nbias_grad)


def solution(mesh):
    split = Mesh(mesh.devices.reshape(4, 4, 2, 2, 4), ("zl", "x", "c", "zh", "y"))
    block = P(("zl", "x"), "c", ("zh", "y"), None)
    return jax.shard_map(
        per_device,
        mesh=split,
        in_specs=(block, block, P(), P(), P(), P(), P()),
        out_specs=(block, P(), P(), P(), P(), P(), P()),
        check_vma=False,
    )
```

```python
import functools
import math

import jax
import jax.numpy as jnp
from jax import lax
from jax.experimental import pallas as pl
from jax.experimental.pallas import tpu as pltpu
from jax.sharding import Mesh, PartitionSpec as P

HEADS = 6
WIN = 8
SHIFT = 4
FAR = -1e30
LANES = 128
PARTS = 8
MAIN = 144
ROWS = MAIN + 8
BEGIN_AT = 3
STEPS_A = 2
STEPS_B = 1
FINISH_AT = 2
F32 = jnp.float32
BF16 = jnp.bfloat16


def dot(a, b):
    return jnp.dot(a, b, preferred_element_type=F32)


def dot_rows(a, b):
    return lax.dot_general(a, b, (((1,), (1,)), ((), ())), preferred_element_type=F32)


def dot_cols(a, b):
    return lax.dot_general(a, b, (((0,), (0,)), ((), ())), preferred_element_type=F32)


def window_kernel(
    flags, gain, nbias, w_cols, w_rows, qbias, proj, near, *rest, steps
):
    far = rest[:-8]
    out, grads, acc_qkv, acc_proj, acc_gain, acc_nb, packed_grad, attended = rest[-8:]
    width = w_rows.shape[0]
    count = WIN**3
    windows_here = near.shape[1] // WIN // steps
    step = pl.program_id(0)
    size = width // HEADS
    factor = size**-0.5
    scale = factor * math.log2(math.e)
    place = lax.broadcasted_iota(jnp.int32, (16, count), 1)
    row = lax.broadcasted_iota(jnp.int32, (16, count), 0)
    ones = jnp.ones((16, count), BF16)

    class Window:
        pass

    def begin(at):
        here = Window()
        here.at = at
        def gathered(lo, hi):
            pieces, start = [], 0
            for piece in far:
                first, last = max(lo - start, 0), min(hi - start, piece.shape[1])
                if first < last:
                    pieces.append(piece[:, first:last].astype(F32))
                start += piece.shape[1]
            return jnp.concatenate(pieces, axis=1)

        wide = windows_here * WIN
        received = gathered(at * WIN, (at + 1) * WIN)
        for j in range(1, steps):
            other = gathered(j * wide + at * WIN, j * wide + (at + 1) * WIN)
            received = jnp.where(step == j, other, received)
        own = near[:, pl.ds(step * wide + at * WIN, WIN)].astype(F32)
        arrived = jnp.concatenate([own, received], axis=0).reshape(count, 2 * width)
        here.upward = arrived[:, :width]
        here.upward_half = here.upward.astype(BF16)
        inputs = arrived[:, LANES:].T[width - LANES :]
        centred = inputs - jnp.mean(inputs, axis=0, keepdims=True)
        here.inverse = lax.rsqrt(jnp.mean(centred * centred, axis=0, keepdims=True) + 1e-5)
        here.normed = centred * here.inverse
        here.hidden = (here.normed * gain[...] + nbias[...]).astype(BF16)
        here.packed = (dot(w_cols[...], here.hidden) + qbias[...]).astype(BF16)
        here.att_grad = dot_rows(proj[...], here.upward_half).astype(BF16)
        last = jnp.where(step == steps - 1, flags[1], 0) if at == windows_here - 1 else 0
        code = (
            4 * flags[0] * ((place >> 8) & 1)
            + 2 * last * ((place >> 5) & 1)
            + flags[2] * ((place >> 2) & 1)
        )
        same = code == row
        here.query_code = jnp.where(same, 1.0, 0.0).astype(BF16)
        here.key_code = jnp.where(same, 0.0, FAR).astype(BF16)
        attended[at, width:, :] = ones
        return here

    def rows_of(kind, head):
        return slice(kind * width + size * head, kind * width + size * (head + 1))

    def score(here, head):
        return dot_cols(
            jnp.concatenate([here.packed[rows_of(1, head)], here.key_code], axis=0),
            jnp.concatenate([here.packed[rows_of(0, head)], here.query_code], axis=0),
        )

    def weigh(scores):
        peak = jnp.max(scores, axis=0, keepdims=True)
        return jnp.exp2((scores - peak) * scale).astype(BF16)

    def values(here, head):
        return jnp.concatenate([here.packed[rows_of(2, head)], ones], axis=0)

    def attend(here, head, expo):
        mixed = dot(values(here, head), expo)
        recip = 1.0 / mixed[size : size + 1]
        result = mixed[:size] * recip
        attended[here.at, rows_of(0, head), :] = result.astype(BF16)
        scaled = (here.att_grad[rows_of(0, head)].astype(F32) * recip).astype(BF16)
        inner = jnp.sum(scaled.astype(F32) * result, axis=0, keepdims=True)
        high = inner.astype(BF16).astype(F32)
        inner_rows = jnp.where(row == 0, -high, jnp.where(row == 1, high - inner, 0.0))
        return scaled, jnp.concatenate([scaled, inner_rows.astype(BF16)], axis=0)

    def pull_back(here, head, expo, scaled, spread):
        score_grad = expo * spread.astype(BF16)
        query, keyset = here.packed[rows_of(0, head)], here.packed[rows_of(1, head)]
        grad_of = packed_grad.at[here.at]
        grad_of[rows_of(2, head), :] = dot_rows(scaled, expo).astype(BF16)
        grad_of[rows_of(0, head), :] = (dot(keyset, score_grad) * factor).astype(BF16)
        grad_of[rows_of(1, head), :] = (dot_rows(score_grad, query).T * factor).astype(BF16)

    def add(total, value, at):
        if at == 0:
            value = jnp.where(step == 0, 0.0, total[...]) + value if steps > 1 else value
            total[...] = value
        else:
            total[...] = total[...] + value

    def finish(here):
        grad_half = packed_grad[here.at]
        add(
            acc_qkv,
            dot_rows(jnp.concatenate([here.hidden, ones], axis=0), grad_half),
            here.at,
        )
        add(acc_proj, dot(attended[here.at], here.upward_half), here.at)
        hidden_grad = dot(w_rows[...], grad_half)
        add(acc_gain, hidden_grad * here.normed, here.at)
        add(acc_nb, hidden_grad, here.at)
        normed_grad = hidden_grad * gain[...]
        first = jnp.mean(normed_grad, axis=0, keepdims=True)
        second = jnp.mean(normed_grad * here.normed, axis=0, keepdims=True)
        change = here.inverse * (normed_grad - first - here.normed * second)
        out[:, here.at * WIN : (here.at + 1) * WIN] = (
            (here.upward + change.T).reshape(WIN, WIN, WIN, width).astype(BF16)
        )

    heads = [(at, head) for at in range(windows_here) for head in range(HEADS)]
    begun = {0: begin(0)}
    scores, earlier = score(begun[0], 0), None
    for number in range(len(heads) + 1):
        inside = number < len(heads)
        at, head = heads[number] if inside else (windows_here, 0)
        if inside and head == BEGIN_AT and at + 1 < windows_here:
            begun[at + 1] = begin(at + 1)
        spread = None
        if earlier is not None:
            before, prior = begun[earlier[0]], earlier[1]
            spread = dot_cols(values(before, prior), earlier[4])
        following = None
        if number + 1 < len(heads):
            next_at, next_head = heads[number + 1]
            following = score(begun[next_at], next_head)
        expo = weigh(scores) if inside else None
        current = (at, head, expo, *attend(begun[at], head, expo)) if inside else None
        if earlier is not None:
            pull_back(before, prior, earlier[2], earlier[3], spread)
        if head == FINISH_AT and 0 < at < windows_here:
            finish(begun[at - 1])
        scores, earlier = following, current
    finish(begun[windows_here - 1])

    def put(at, value):
        done = 0
        while done < value.shape[0]:
            part, inside = divmod(at + done, MAIN)
            rows = min(value.shape[0] - done, MAIN - inside)
            grads[part, inside : inside + rows, :] = value[done : done + rows]
            done += rows

    def put_small(at, value):
        grads[at // 2, MAIN + at % 2, : value.shape[1]] = value[0]

    def over_tokens(value):
        folded = value[:, :LANES]
        for j in range(1, count // LANES):
            folded = folded + value[:, j * LANES : (j + 1) * LANES]
        return jnp.sum(folded.T, axis=0, keepdims=True)

    qkv = acc_qkv[...]
    prj = acc_proj[...]
    for j in range(4):
        put(width * j, qkv[:width, j * LANES : (j + 1) * LANES])
    put(width * 4, prj[:width, :LANES])
    put(
        width * 5,
        jnp.concatenate([qkv[:width, 4 * LANES :], prj[:width, LANES:]], axis=1),
    )
    grads[:, MAIN:, :] = jnp.zeros_like(grads[:, MAIN:, :])
    for j in range(5):
        put_small(j, qkv[width : width + 1, j * LANES : (j + 1) * LANES])
    small = [prj[width : width + 1], over_tokens(acc_gain[...]), over_tokens(acc_nb[...])]
    for j, value in enumerate(small):
        put_small(8 + 2 * j, value[:, :LANES])
        put_small(9 + 2 * j, value[:, LANES:])


def windows(steps, flags, weights, near, *far):
    depth, width_y, depth_z, wide = near.shape
    depth += far[0].shape[0]
    width = wide // 2
    count = WIN**3
    operands = (*weights, near, *far)
    return pl.pallas_call(
        functools.partial(window_kernel, steps=steps),
        grid=(steps,),
        in_specs=[pl.BlockSpec(memory_space=pltpu.SMEM)]
        + [pl.BlockSpec(memory_space=pltpu.VMEM)] * len(operands),
        out_specs=[
            pl.BlockSpec((depth, width_y // steps, depth_z, width), lambda i: (0, i, 0, 0)),
            pl.BlockSpec((PARTS, ROWS, LANES), lambda i: (0, 0, 0)),
        ],
        out_shape=[
            jax.ShapeDtypeStruct((depth, width_y, depth_z, width), BF16),
            jax.ShapeDtypeStruct((PARTS, ROWS, LANES), F32),
        ],
        scratch_shapes=[
            pltpu.VMEM((width + 16, 3 * width), F32),
            pltpu.VMEM((width + 16, width), F32),
            pltpu.VMEM((width, count), F32),
            pltpu.VMEM((width, count), F32),
            pltpu.VMEM((width_y // WIN // steps, 3 * width, count), BF16),
            pltpu.VMEM((width_y // WIN // steps, width + 16, count), BF16),
        ],
        compiler_params=pltpu.CompilerParams(vmem_limit_bytes=48 * 2**20),
        cost_estimate=pl.CostEstimate(
            flops=20 * 10**9, transcendentals=4 * 10**6, bytes_accessed=4 * 10**6
        ),
        name="window_grads",
    )(flags, *operands)


def swapped(value, axis, bit):
    axes = (axis,) if isinstance(axis, str) else axis
    count = math.prod(lax.axis_size(name) for name in axes)
    return lax.ppermute(value, axis, [(a, a ^ bit) for a in range(count)])


def coded(value):
    small = value[:, MAIN:]
    high = lax.reduce_precision(small, 8, 7)
    return jnp.concatenate([value[:, :MAIN], high, small - high], axis=1).astype(BF16)


def decoded(value):
    wide = value.astype(F32)
    small = wide[:, MAIN:ROWS] + wide[:, ROWS:]
    return jnp.concatenate([wide[:, :MAIN], small], axis=1)


def halve(value, axis):
    half = value.shape[0] // 2
    upper = lax.axis_index(axis) % 2
    kept = lax.dynamic_slice_in_dim(value, upper * half, half, 0)
    given = lax.dynamic_slice_in_dim(value, (1 - upper) * half, half, 0)
    return kept + decoded(swapped(coded(given), axis, 1))


def quarter(value, axis):
    part = value.shape[0] // 4
    at = lax.axis_index(axis)
    sent = coded(value)
    total = lax.dynamic_slice_in_dim(value, at * part, part, 0)
    for bits in (2, 1, 3):
        given = lax.dynamic_slice_in_dim(sent, (at ^ bits) * part, part, 0)
        total = total + decoded(swapped(given, axis, bits))
    return total


def sum_of_two(value, axes, bit):
    sent = coded(value)
    return decoded(sent) + decoded(swapped(sent, axes, bit))


def sum_of_four(value, axes, first, second):
    sent = coded(value)
    both = swapped(sent, axes, first ^ second)
    one, two = swapped(sent, axes, first), swapped(sent, axes, second)
    return (decoded(sent) + decoded(one)) + (decoded(two) + decoded(both))


def join_four(value, axis):
    at = lax.axis_index(axis)
    odd, upper = at % 2 == 1, at >= 2
    far, one, three = (swapped(value, axis, bits) for bits in (2, 1, 3))
    flat = [
        jnp.where(odd, one, value),
        jnp.where(odd, value, one),
        jnp.where(odd, three, far),
        jnp.where(odd, far, three),
    ]
    return jnp.concatenate([jnp.where(upper, flat[j ^ 2], flat[j]) for j in range(4)], axis=0)


def summed_everywhere(value):
    value = quarter(halve(value, "c"), "y")
    value = sum_of_four(value, ("x",), 1, 2)
    value = sum_of_two(value, ("zl", "zh"), 2)
    value = sum_of_four(value, ("zl", "zh"), 4, 1)
    return join_four(coded(value), "y")


def unpack_kernel(upper, mine, other, qkv, proj, qbias, pbias, gain, nbias, *, width, factor):
    here = upper[0] == 1
    first = decoded(jnp.where(here, other[...], mine[...])) * factor
    second = decoded(jnp.where(here, mine[...], other[...])) * factor
    both = jnp.concatenate([first, second], axis=0)
    main = both[:, :MAIN].reshape(PARTS * MAIN, LANES)
    block = lambda j: main[width * j : width * (j + 1)]
    for j in range(4):
        qkv[:, j * LANES : (j + 1) * LANES] = block(j)
    rest = block(5)
    qkv[:, 4 * LANES :] = rest[:, : width - LANES]
    proj[:, :LANES] = block(4)
    proj[:, LANES:] = rest[:, width - LANES :]

    def put(target, at):
        for j in range(-(-target.shape[0] // LANES)):
            wide = min(LANES, target.shape[0] - j * LANES)
            line = both[(at + j) // 2, MAIN + (at + j) % 2]
            target[j * LANES : j * LANES + wide] = line[:wide]

    for target, at in ((qbias, 0), (pbias, 8), (gain, 10), (nbias, 12)):
        put(target, at)


def unpacked(value, axis, width, factor):
    shapes = [(width, 3 * width), (width, width), (3 * width,), (width,), (width,), (width,)]
    return pl.pallas_call(
        functools.partial(unpack_kernel, width=width, factor=factor),
        in_specs=[pl.BlockSpec(memory_space=pltpu.SMEM)]
        + [pl.BlockSpec(memory_space=pltpu.VMEM)] * 2,
        out_specs=[pl.BlockSpec(memory_space=pltpu.VMEM)] * 6,
        out_shape=[jax.ShapeDtypeStruct(shape, F32) for shape in shapes],
        compiler_params=pltpu.CompilerParams(vmem_limit_bytes=16 * 2**20),
        name="unpack_sums",
    )(lax.axis_index(axis).reshape(1), value, swapped(value, axis, 1))


def passed_back(value, axes):
    sizes = [lax.axis_size(axis) for axis in axes]
    count = math.prod(sizes)
    return lax.ppermute(value, axes, [(a, (a - 1) % count) for a in range(count)])


def passed_back_both(value, first, second):
    ones = [lax.axis_size(axis) for axis in first]
    twos = [lax.axis_size(axis) for axis in second]
    n, m = math.prod(ones), math.prod(twos)
    pairs = [
        (a * m + b, ((a - 1) % n) * m + (b - 1) % m) for a in range(n) for b in range(m)
    ]
    return lax.ppermute(value, first + second, pairs)


def per_device(tokens, upstream, norm_gain, norm_bias, qkv_weight, qkv_bias, proj_weight):
    gx, gy, gz = ("zl", "x"), ("c",), ("zh", "y")
    width = tokens.shape[3]
    both = jnp.concatenate([upstream, tokens], axis=3)
    a_z, b_z = slice(SHIFT, SHIFT + WIN), slice(SHIFT + WIN, None)
    came_a = passed_back(both[:SHIFT, SHIFT:, a_z], gx)
    came_y = passed_back(both[:, :SHIFT], gy)
    came_ay = passed_back(came_y[:SHIFT, :, a_z], gx)
    both = jnp.concatenate([both[:, SHIFT:], came_y], axis=1)
    came_b = passed_back(both[:SHIFT, :, b_z], gx)
    came_z = passed_back(both[SHIFT:, :, :SHIFT], gz)
    came_xz = passed_back_both(both[:SHIFT, :, :SHIFT], gx, gz)
    def is_last(axes):
        at = jnp.int32(0)
        count = 1
        for axis in axes:
            at = at * lax.axis_size(axis) + lax.axis_index(axis)
            count *= lax.axis_size(axis)
        return (at == count - 1).astype(jnp.int32)

    last_x, last_y, last_z = is_last(gx), is_last(gy), is_last(gz)
    weights = (
        norm_gain.reshape(-1, 1),
        norm_bias.reshape(-1, 1),
        qkv_weight.T,
        qkv_weight,
        qkv_bias.reshape(-1, 1),
        proj_weight,
    )
    out_a, grads_a = windows(
        STEPS_A,
        jnp.stack([last_x, last_y, 0 * last_z]), weights, both[SHIFT:, :, a_z], came_a, came_ay
    )
    out_b, grads_b = windows(
        STEPS_B,
        jnp.stack([last_x, last_y, last_z]),
        weights,
        jnp.concatenate([both[SHIFT:, :, b_z], came_z], axis=2),
        jnp.concatenate([came_b, came_xz], axis=2),
    )
    token_grad = jnp.concatenate([out_a, out_b], axis=2)
    devices = math.prod(lax.axis_size(axis) for axis in gx + gy + gz)
    factor = float(math.prod(tokens.shape[:3]) * devices) ** (-0.5)
    quarters = summed_everywhere(grads_a + grads_b)
    qkv_grad, proj_grad, qbias_grad, pbias_grad, gain_grad, nbias_grad = unpacked(
        quarters, "c", width, factor
    )
    return (token_grad, qkv_grad, qbias_grad, proj_grad, pbias_grad, gain_grad, nbias_grad)


def solution(mesh):
    split = Mesh(mesh.devices.reshape(4, 4, 2, 2, 4), ("zl", "x", "c", "zh", "y"))
    block = P(("zl", "x"), "c", ("zh", "y"), None)
    return jax.shard_map(
        per_device,
        mesh=split,
        in_specs=(block, block, P(), P(), P(), P(), P()),
        out_specs=(block, P(), P(), P(), P(), P(), P()),
        check_vma=False,
    )
```

```python
import functools
import math

import jax
import jax.numpy as jnp
from jax import lax
from jax.experimental import pallas as pl
from jax.experimental.pallas import tpu as pltpu
from jax.sharding import Mesh, PartitionSpec as P

HEADS = 6
WIN = 8
SHIFT = 4
FAR = -1e30
LANES = 128
PARTS = 8
MAIN = 144
ROWS = MAIN + 8
BEGIN_AT = 3
STEPS_A = 1
STEPS_B = 2
FINISH_AT = 2
F32 = jnp.float32
BF16 = jnp.bfloat16


def dot(a, b):
    return jnp.dot(a, b, preferred_element_type=F32)


def dot_rows(a, b):
    return lax.dot_general(a, b, (((1,), (1,)), ((), ())), preferred_element_type=F32)


def dot_cols(a, b):
    return lax.dot_general(a, b, (((0,), (0,)), ((), ())), preferred_element_type=F32)


def window_kernel(
    flags, gain, nbias, w_cols, w_rows, qbias, proj, near, *rest, steps
):
    far = rest[:-8]
    out, grads, acc_qkv, acc_proj, acc_gain, acc_nb, packed_grad, attended = rest[-8:]
    width = w_rows.shape[0]
    count = WIN**3
    windows_here = near.shape[1] // WIN // steps
    step = pl.program_id(0)
    size = width // HEADS
    factor = size**-0.5
    scale = factor * math.log2(math.e)
    place = lax.broadcasted_iota(jnp.int32, (16, count), 1)
    row = lax.broadcasted_iota(jnp.int32, (16, count), 0)
    ones = jnp.ones((16, count), BF16)

    class Window:
        pass

    def begin(at):
        here = Window()
        here.at = at
        def gathered(lo, hi):
            pieces, start = [], 0
            for piece in far:
                first, last = max(lo - start, 0), min(hi - start, piece.shape[1])
                if first < last:
                    pieces.append(piece[:, first:last].astype(F32))
                start += piece.shape[1]
            return jnp.concatenate(pieces, axis=1)

        wide = windows_here * WIN
        received = gathered(at * WIN, (at + 1) * WIN)
        for j in range(1, steps):
            other = gathered(j * wide + at * WIN, j * wide + (at + 1) * WIN)
            received = jnp.where(step == j, other, received)
        own = near[:, pl.ds(step * wide + at * WIN, WIN)].astype(F32)
        arrived = jnp.concatenate([own, received], axis=0).reshape(count, 2 * width)
        here.upward = arrived[:, :width]
        here.upward_half = here.upward.astype(BF16)
        inputs = arrived[:, LANES:].T[width - LANES :]
        centred = inputs - jnp.mean(inputs, axis=0, keepdims=True)
        here.inverse = lax.rsqrt(jnp.mean(centred * centred, axis=0, keepdims=True) + 1e-5)
        here.normed = centred * here.inverse
        here.hidden = (here.normed * gain[...] + nbias[...]).astype(BF16)
        here.packed = (dot(w_cols[...], here.hidden) + qbias[...]).astype(BF16)
        here.att_grad = dot_rows(proj[...], here.upward_half).astype(BF16)
        last = jnp.where(step == steps - 1, flags[1], 0) if at == windows_here - 1 else 0
        code = (
            4 * flags[0] * ((place >> 8) & 1)
            + 2 * last * ((place >> 5) & 1)
            + flags[2] * ((place >> 2) & 1)
        )
        same = code == row
        here.query_code = jnp.where(same, 1.0, 0.0).astype(BF16)
        here.key_code = jnp.where(same, 0.0, FAR).astype(BF16)
        attended[at, width:, :] = ones
        return here

    def rows_of(kind, head):
        return slice(kind * width + size * head, kind * width + size * (head + 1))

    def score(here, head):
        return dot_cols(
            jnp.concatenate([here.packed[rows_of(1, head)], here.key_code], axis=0),
            jnp.concatenate([here.packed[rows_of(0, head)], here.query_code], axis=0),
        )

    def weigh(scores):
        peak = jnp.max(scores, axis=0, keepdims=True)
        return jnp.exp2((scores - peak) * scale).astype(BF16)

    def values(here, head):
        return jnp.concatenate([here.packed[rows_of(2, head)], ones], axis=0)

    def attend(here, head, expo):
        mixed = dot(values(here, head), expo)
        recip = 1.0 / mixed[size : size + 1]
        result = mixed[:size] * recip
        attended[here.at, rows_of(0, head), :] = result.astype(BF16)
        scaled = (here.att_grad[rows_of(0, head)].astype(F32) * recip).astype(BF16)
        inner = jnp.sum(scaled.astype(F32) * result, axis=0, keepdims=True)
        high = inner.astype(BF16).astype(F32)
        inner_rows = jnp.where(row == 0, -high, jnp.where(row == 1, high - inner, 0.0))
        return scaled, jnp.concatenate([scaled, inner_rows.astype(BF16)], axis=0)

    def pull_back(here, head, expo, scaled, spread):
        score_grad = expo * spread.astype(BF16)
        query, keyset = here.packed[rows_of(0, head)], here.packed[rows_of(1, head)]
        grad_of = packed_grad.at[here.at]
        grad_of[rows_of(2, head), :] = dot_rows(scaled, expo).astype(BF16)
        grad_of[rows_of(0, head), :] = (dot(keyset, score_grad) * factor).astype(BF16)
        grad_of[rows_of(1, head), :] = (dot_rows(score_grad, query).T * factor).astype(BF16)

    def add(total, value, at):
        if at == 0:
            value = jnp.where(step == 0, 0.0, total[...]) + value if steps > 1 else value
            total[...] = value
        else:
            total[...] = total[...] + value

    def finish(here):
        grad_half = packed_grad[here.at]
        add(
            acc_qkv,
            dot_rows(jnp.concatenate([here.hidden, ones], axis=0), grad_half),
            here.at,
        )
        add(acc_proj, dot(attended[here.at], here.upward_half), here.at)
        hidden_grad = dot(w_rows[...], grad_half)
        add(acc_gain, hidden_grad * here.normed, here.at)
        add(acc_nb, hidden_grad, here.at)
        normed_grad = hidden_grad * gain[...]
        first = jnp.mean(normed_grad, axis=0, keepdims=True)
        second = jnp.mean(normed_grad * here.normed, axis=0, keepdims=True)
        change = here.inverse * (normed_grad - first - here.normed * second)
        out[:, here.at * WIN : (here.at + 1) * WIN] = (
            (here.upward + change.T).reshape(WIN, WIN, WIN, width).astype(BF16)
        )

    heads = [(at, head) for at in range(windows_here) for head in range(HEADS)]
    begun = {0: begin(0)}
    scores, earlier = score(begun[0], 0), None
    for number in range(len(heads) + 1):
        inside = number < len(heads)
        at, head = heads[number] if inside else (windows_here, 0)
        if inside and head == BEGIN_AT and at + 1 < windows_here:
            begun[at + 1] = begin(at + 1)
        spread = None
        if earlier is not None:
            before, prior = begun[earlier[0]], earlier[1]
            spread = dot_cols(values(before, prior), earlier[4])
        following = None
        if number + 1 < len(heads):
            next_at, next_head = heads[number + 1]
            following = score(begun[next_at], next_head)
        expo = weigh(scores) if inside else None
        current = (at, head, expo, *attend(begun[at], head, expo)) if inside else None
        if earlier is not None:
            pull_back(before, prior, earlier[2], earlier[3], spread)
        if head == FINISH_AT and 0 < at < windows_here:
            finish(begun[at - 1])
        scores, earlier = following, current
    finish(begun[windows_here - 1])

    def put(at, value):
        done = 0
        while done < value.shape[0]:
            part, inside = divmod(at + done, MAIN)
            rows = min(value.shape[0] - done, MAIN - inside)
            grads[part, inside : inside + rows, :] = value[done : done + rows]
            done += rows

    def put_small(at, value):
        grads[at // 2, MAIN + at % 2, : value.shape[1]] = value[0]

    def over_tokens(value):
        folded = value[:, :LANES]
        for j in range(1, count // LANES):
            folded = folded + value[:, j * LANES : (j + 1) * LANES]
        return jnp.sum(folded.T, axis=0, keepdims=True)

    qkv = acc_qkv[...]
    prj = acc_proj[...]
    for j in range(4):
        put(width * j, qkv[:width, j * LANES : (j + 1) * LANES])
    put(width * 4, prj[:width, :LANES])
    put(
        width * 5,
        jnp.concatenate([qkv[:width, 4 * LANES :], prj[:width, LANES:]], axis=1),
    )
    grads[:, MAIN:, :] = jnp.zeros_like(grads[:, MAIN:, :])
    for j in range(5):
        put_small(j, qkv[width : width + 1, j * LANES : (j + 1) * LANES])
    small = [prj[width : width + 1], over_tokens(acc_gain[...]), over_tokens(acc_nb[...])]
    for j, value in enumerate(small):
        put_small(8 + 2 * j, value[:, :LANES])
        put_small(9 + 2 * j, value[:, LANES:])


def windows(steps, flags, weights, near, *far):
    depth, width_y, depth_z, wide = near.shape
    depth += far[0].shape[0]
    width = wide // 2
    count = WIN**3
    operands = (*weights, near, *far)
    return pl.pallas_call(
        functools.partial(window_kernel, steps=steps),
        grid=(steps,),
        in_specs=[pl.BlockSpec(memory_space=pltpu.SMEM)]
        + [pl.BlockSpec(memory_space=pltpu.VMEM)] * len(operands),
        out_specs=[
            pl.BlockSpec((depth, width_y // steps, depth_z, width), lambda i: (0, i, 0, 0)),
            pl.BlockSpec((PARTS, ROWS, LANES), lambda i: (0, 0, 0)),
        ],
        out_shape=[
            jax.ShapeDtypeStruct((depth, width_y, depth_z, width), BF16),
            jax.ShapeDtypeStruct((PARTS, ROWS, LANES), F32),
        ],
        scratch_shapes=[
            pltpu.VMEM((width + 16, 3 * width), F32),
            pltpu.VMEM((width + 16, width), F32),
            pltpu.VMEM((width, count), F32),
            pltpu.VMEM((width, count), F32),
            pltpu.VMEM((width_y // WIN // steps, 3 * width, count), BF16),
            pltpu.VMEM((width_y // WIN // steps, width + 16, count), BF16),
        ],
        compiler_params=pltpu.CompilerParams(vmem_limit_bytes=48 * 2**20),
        cost_estimate=pl.CostEstimate(
            flops=20 * 10**9, transcendentals=4 * 10**6, bytes_accessed=4 * 10**6
        ),
        name="window_grads",
    )(flags, *operands)


def swapped(value, axis, bit):
    axes = (axis,) if isinstance(axis, str) else axis
    count = math.prod(lax.axis_size(name) for name in axes)
    return lax.ppermute(value, axis, [(a, a ^ bit) for a in range(count)])


def coded(value):
    small = value[:, MAIN:]
    low = small - lax.reduce_precision(small, 8, 7)
    return jnp.concatenate([value, low], axis=1).astype(BF16)


def decoded(value):
    wide = value.astype(F32)
    return wide[:, :ROWS] + jnp.pad(wide[:, ROWS:], ((0, 0), (MAIN, 0), (0, 0)))


def halve(value, axis):
    half = value.shape[0] // 2
    upper = lax.axis_index(axis) % 2
    kept = lax.dynamic_slice_in_dim(value, upper * half, half, 0)
    given = lax.dynamic_slice_in_dim(value, (1 - upper) * half, half, 0)
    return kept + decoded(swapped(coded(given), axis, 1))


def quarter(value, axis):
    part = value.shape[0] // 4
    at = lax.axis_index(axis)
    sent = coded(value)
    total = lax.dynamic_slice_in_dim(value, at * part, part, 0)
    for bits in (2, 1, 3):
        given = lax.dynamic_slice_in_dim(sent, (at ^ bits) * part, part, 0)
        total = total + decoded(swapped(given, axis, bits))
    return total


def sum_of_two(value, axes, bit):
    sent = coded(value)
    return decoded(sent) + decoded(swapped(sent, axes, bit))


def sum_of_four(value, axes, first, second):
    sent = coded(value)
    both = swapped(sent, axes, first ^ second)
    one, two = swapped(sent, axes, first), swapped(sent, axes, second)
    return (decoded(sent) + decoded(one)) + (decoded(two) + decoded(both))


def join_four(value, axis):
    at = lax.axis_index(axis)
    odd, upper = at % 2 == 1, at >= 2
    far, one, three = (swapped(value, axis, bits) for bits in (2, 1, 3))
    flat = [
        jnp.where(odd, one, value),
        jnp.where(odd, value, one),
        jnp.where(odd, three, far),
        jnp.where(odd, far, three),
    ]
    return jnp.concatenate([jnp.where(upper, flat[j ^ 2], flat[j]) for j in range(4)], axis=0)


def summed_everywhere(value):
    value = quarter(halve(value, "c"), "y")
    value = sum_of_four(value, ("x",), 1, 2)
    value = sum_of_two(value, ("zl", "zh"), 2)
    value = sum_of_four(value, ("zl", "zh"), 4, 1)
    return join_four(coded(value), "y")


def opened(value):
    wide = value.astype(F32)
    small = wide[:, MAIN:ROWS] + wide[:, ROWS:]
    return jnp.concatenate([wide[:, :MAIN], small], axis=1)


def unpack_kernel(upper, mine, other, qkv, proj, qbias, pbias, gain, nbias, *, width, factor):
    here = upper[0] == 1
    first = opened(jnp.where(here, other[...], mine[...])) * factor
    second = opened(jnp.where(here, mine[...], other[...])) * factor
    both = jnp.concatenate([first, second], axis=0)
    main = both[:, :MAIN].reshape(PARTS * MAIN, LANES)
    block = lambda j: main[width * j : width * (j + 1)]
    for j in range(4):
        qkv[:, j * LANES : (j + 1) * LANES] = block(j)
    rest = block(5)
    qkv[:, 4 * LANES :] = rest[:, : width - LANES]
    proj[:, :LANES] = block(4)
    proj[:, LANES:] = rest[:, width - LANES :]

    def put(target, at):
        for j in range(-(-target.shape[0] // LANES)):
            wide = min(LANES, target.shape[0] - j * LANES)
            line = both[(at + j) // 2, MAIN + (at + j) % 2]
            target[j * LANES : j * LANES + wide] = line[:wide]

    for target, at in ((qbias, 0), (pbias, 8), (gain, 10), (nbias, 12)):
        put(target, at)


def unpacked(value, axis, width, factor):
    shapes = [(width, 3 * width), (width, width), (3 * width,), (width,), (width,), (width,)]
    return pl.pallas_call(
        functools.partial(unpack_kernel, width=width, factor=factor),
        in_specs=[pl.BlockSpec(memory_space=pltpu.SMEM)]
        + [pl.BlockSpec(memory_space=pltpu.VMEM)] * 2,
        out_specs=[pl.BlockSpec(memory_space=pltpu.VMEM)] * 6,
        out_shape=[jax.ShapeDtypeStruct(shape, F32) for shape in shapes],
        compiler_params=pltpu.CompilerParams(vmem_limit_bytes=16 * 2**20),
        name="unpack_sums",
    )(lax.axis_index(axis).reshape(1), value, swapped(value, axis, 1))


def passed_back(value, axes):
    sizes = [lax.axis_size(axis) for axis in axes]
    count = math.prod(sizes)
    return lax.ppermute(value, axes, [(a, (a - 1) % count) for a in range(count)])


def passed_back_both(value, first, second):
    ones = [lax.axis_size(axis) for axis in first]
    twos = [lax.axis_size(axis) for axis in second]
    n, m = math.prod(ones), math.prod(twos)
    pairs = [
        (a * m + b, ((a - 1) % n) * m + (b - 1) % m) for a in range(n) for b in range(m)
    ]
    return lax.ppermute(value, first + second, pairs)


def per_device(tokens, upstream, norm_gain, norm_bias, qkv_weight, qkv_bias, proj_weight):
    gx, gy, gz = ("zl", "x"), ("c",), ("zh", "y")
    width = tokens.shape[3]
    both = jnp.concatenate([upstream, tokens], axis=3)
    a_z, b_z = slice(SHIFT, SHIFT + WIN), slice(SHIFT + WIN, None)
    came_a = passed_back(both[:SHIFT, SHIFT:, a_z], gx)
    came_y = passed_back(both[:, :SHIFT], gy)
    came_ay = passed_back(came_y[:SHIFT, :, a_z], gx)
    both = jnp.concatenate([both[:, SHIFT:], came_y], axis=1)
    came_b = passed_back(both[:SHIFT, :, b_z], gx)
    came_z = passed_back(both[SHIFT:, :, :SHIFT], gz)
    came_xz = passed_back_both(both[:SHIFT, :, :SHIFT], gx, gz)
    def is_last(axes):
        at = jnp.int32(0)
        count = 1
        for axis in axes:
            at = at * lax.axis_size(axis) + lax.axis_index(axis)
            count *= lax.axis_size(axis)
        return (at == count - 1).astype(jnp.int32)

    last_x, last_y, last_z = is_last(gx), is_last(gy), is_last(gz)
    weights = (
        norm_gain.reshape(-1, 1),
        norm_bias.reshape(-1, 1),
        qkv_weight.T,
        qkv_weight,
        qkv_bias.reshape(-1, 1),
        proj_weight,
    )
    out_a, grads_a = windows(
        STEPS_A,
        jnp.stack([last_x, last_y, 0 * last_z]), weights, both[SHIFT:, :, a_z], came_a, came_ay
    )
    out_b, grads_b = windows(
        STEPS_B,
        jnp.stack([last_x, last_y, last_z]),
        weights,
        jnp.concatenate([both[SHIFT:, :, b_z], came_z], axis=2),
        jnp.concatenate([came_b, came_xz], axis=2),
    )
    token_grad = jnp.concatenate([out_a, out_b], axis=2)
    devices = math.prod(lax.axis_size(axis) for axis in gx + gy + gz)
    factor = float(math.prod(tokens.shape[:3]) * devices) ** (-0.5)
    quarters = summed_everywhere(grads_a + grads_b)
    qkv_grad, proj_grad, qbias_grad, pbias_grad, gain_grad, nbias_grad = unpacked(
        quarters, "c", width, factor
    )
    return (token_grad, qkv_grad, qbias_grad, proj_grad, pbias_grad, gain_grad, nbias_grad)


def solution(mesh):
    split = Mesh(mesh.devices.reshape(4, 4, 2, 2, 4), ("zl", "x", "c", "zh", "y"))
    block = P(("zl", "x"), "c", ("zh", "y"), None)
    return jax.shard_map(
        per_device,
        mesh=split,
        in_specs=(block, block, P(), P(), P(), P(), P()),
        out_specs=(block, P(), P(), P(), P(), P(), P()),
        check_vma=False,
    )
```
